256 devices in a mesh: ctx: 16 (over z, y_hi), grp: 16 (over y_lo, x, core).
Axes of the slice: x: 4, y: 4 (y_hi: 2, y_lo: 2; y = y_hi * 2 + y_lo), z: 8, core: 2. Of those that a mesh axis runs over, the one named last changes fastest.
Arguments:
- q_latent: bfloat16 [4096, 1536], P('ctx'), may hold values from -210 to 210
- kv_latent: bfloat16 [4096, 576], P('ctx'), may hold values from -6 to 6
- kv_gain: float32 [512], replicated, may hold values from 0.1 to 1.9
- q_weight: bfloat16 [1536, 24576], P('ctx', 'grp'), may hold values from -0.15625 to 0.15625
- kv_weight: bfloat16 [512, 32768], P('ctx', 'grp'), may hold values from -0.25 to 0.25
- out_weight: bfloat16 [16384, 7168], P('grp', 'ctx'), may hold values from -0.0625 to 0.0625
- documents: int32 [4096], replicated, may hold values from 0 to 7, never falling along the last dimension, each value on 1 to 1024 neighbouring positions
Outputs:
- mixed: bfloat16 [4096, 7168], P('ctx', 'grp')
The draws below stay inside these ranges and needn't reach their ends.
All inputs are finite; a program needn't handle non-finite values.
Results may differ from the reference program's by a relative error of at most 0.018.
Values may be sent and summed in bfloat16 or wider, within the bound.
A program may use at most 64 MiB of HBM per device.

```python
import math
import jax
import jax.numpy as jnp
import numpy as np
from jax import lax

D = 7168
QL = 1536
KL = 512
NOPE = 128
ROPE = 64
VDIM = 128
HEAD_DEV = 8
TOK_DEV = 256
HEADS = 128
TOKENS = 4096
N_CTX = 16
N_GRP = 16


def draw_q_latent(key, part):
    sample = jnp.clip(jax.random.normal(key, (TOKENS, QL), jnp.float32), -6.0, 6.0)
    return sample.astype(jnp.bfloat16)


def with_spikes(values, own_key, source, target, blocks, factor):
    owner, partner = [(jnp.arange(values.shape[axis_at]) // (values.shape[axis_at] // blocks)).reshape([-1 if axis == axis_at else 1 for axis in range(values.ndim)]) for axis_at in (source, target)]
    chosen = jax.random.permutation(own_key, blocks)[partner]
    strong = (owner == chosen) | (owner == (partner + blocks // 2) % blocks)
    return jnp.where(strong, factor * values, values)


def level_of(stream_key, extent, pieces, low, top_value):
    def one(position, blocks):
        heights = jax.random.uniform(jax.random.fold_in(jax.random.fold_in(stream_key, 6), position), (blocks,), jnp.float32, low / len(pieces), top_value / len(pieces))
        return jnp.repeat(jnp.exp(heights), extent[position] // blocks).reshape((-1,) + (1,) * (len(extent) - position - 1))

    factor_of = one(*pieces[0])
    for cut in pieces[1:]:
        factor_of = factor_of * one(*cut)
    return factor_of


def split_up(number_of, total, most, skew):
    portions = [(1 << 20) // math.isqrt(grade ** skew) + 1 for grade in range(2, number_of + 1)]
    surplus, given = total - most - (number_of - 1), [1] * (number_of - 1)
    while surplus > 0:
        candidates = [i for i in range(number_of - 1) if given[i] < most]
        pool, remaining = sum([portions[i] for i in candidates]), surplus
        for i in candidates:
            more = min(most - given[i], max(1, remaining * portions[i] // pool), surplus)
            given[i] = given[i] + more
            surplus = surplus - more
    return np.array([most] + given)


def ragged(own_key, count, total, most, lean):
    if count == 2:
        one = jax.random.randint(own_key, (), max(1, total - most), min(most, total - 1) + 1)
        return jnp.stack([one, total - one])
    sizes = jnp.asarray(split_up(count, total, most, lean), jnp.int32)
    couples = (count - 1) // 2
    donor, sink = sizes[1:1 + 2 * couples:2], sizes[2:2 + 2 * couples:2]
    margin = jnp.minimum(donor - 1, most - sink)
    moved = jax.random.randint(jax.random.fold_in(own_key, 1), (couples,), 0, 1 << 20) % (margin + 1)
    sizes = sizes.at[1:1 + 2 * couples:2].set(donor - moved).at[2:2 + 2 * couples:2].set(sink + moved)
    return sizes[jax.random.permutation(jax.random.fold_in(own_key, 2), count)]


def scatter_about(own_key, shape, spread, limit, shards=(), held_as=jnp.bfloat16):
    gain = level_of(own_key, shape, shards, -0.22, 0.18) if shards else 1.0
    drawn = jax.random.normal(own_key, shape, jnp.float32) * spread * gain
    return jnp.minimum(jnp.maximum(drawn, -limit), limit).astype(held_as)


def noise_with(rng, shape, width, reach, split, heavy, kind=jnp.bfloat16):
    values = width * jax.random.normal(rng, shape, jnp.float32)
    if split:
        values = values * level_of(rng, shape, split, -0.22, 0.18)
    return jnp.clip(with_spikes(values, jax.random.fold_in(rng, 3), *heavy), -reach, reach).astype(kind)


def setup_inputs(seed: int = 0) -> dict:
    seeds = jax.random.split(jax.random.key(seed), 8)
    q_latent = draw_q_latent(jax.random.fold_in(seeds[7], 71), 0)
    kv_latent = scatter_about(seeds[1], (TOKENS, KL + ROPE), 1.0, 6.0, ((0, 16),))
    kv_gain = jnp.clip(1.0 + 0.18 * jax.random.normal(seeds[2], (KL,), jnp.float32), 0.1, 1.9)
    q_weight = scatter_about(seeds[3], (QL, HEADS * (NOPE + ROPE)), QL ** -0.5, 0.15625, ((0, 16), (1, 16)))
    kv_weight = scatter_about(seeds[4], (KL, HEADS * (NOPE + VDIM)), KL ** -0.5, 0.25, ((0, 16), (1, 16)))
    out_weight = noise_with(seeds[5], (HEADS * VDIM, D), (HEADS * VDIM) ** -0.5, 0.0625, ((0, 16), (1, 16)), (0, 1, 16, 2.0))
    documents = jnp.searchsorted(jnp.cumsum(ragged(seeds[6], N_CTX // 2, TOKENS, 4 * TOK_DEV, 2)), jnp.arange(TOKENS), side="right").astype(jnp.int32)
    return dict(q_latent=q_latent, kv_latent=kv_latent, kv_gain=kv_gain, q_weight=q_weight, kv_weight=kv_weight, out_weight=out_weight, documents=documents)


epsilon = 1e-06

def rotate(inputs, positions):
    half_width = inputs.shape[-1] // 2
    inverse = 10000.0 ** (-2.0 * jnp.arange(half_width, dtype=jnp.float32) / inputs.shape[-1])
    angles = positions.astype(jnp.float32)[:, None] * inverse[None, :]
    shape = (angles.shape[0],) + (1,) * (inputs.ndim - 2) + (half_width,)
    cosine = jnp.cos(angles).reshape(shape)
    sine_part = jnp.sin(angles).reshape(shape)
    front_half = inputs[..., :half_width]
    back_half = inputs[..., half_width:]
    return jnp.concatenate([front_half * cosine - back_half * sine_part, back_half * cosine + front_half * sine_part], axis=-1)

def reference(q_latent, kv_latent, kv_gain, q_weight, kv_weight, out_weight, documents):
    tokens = q_latent.shape[0]
    head_count = HEAD_DEV * N_GRP
    positions = jnp.arange(tokens, dtype=jnp.int32)
    query = jnp.dot(q_latent, q_weight, preferred_element_type=jnp.float32).reshape(tokens, head_count, NOPE + ROPE)
    query_nope = query[..., :NOPE].astype(jnp.bfloat16)
    query_rope = rotate(query[..., NOPE:], positions).astype(jnp.bfloat16)
    latent = kv_latent[:, :KL].astype(jnp.float32)
    normed = latent * lax.rsqrt(lax.optimization_barrier(jnp.mean(latent * latent, axis=-1, keepdims=True)) + epsilon) * kv_gain.astype(jnp.float32)
    normed = normed.astype(jnp.bfloat16)
    key_rope = rotate(kv_latent[:, KL:].astype(jnp.float32), positions).astype(jnp.bfloat16)
    key_value = jnp.dot(normed, kv_weight, preferred_element_type=jnp.float32).astype(jnp.bfloat16)
    key_value = key_value.reshape(tokens, head_count, NOPE + VDIM)
    key_nope = jnp.pad(key_value[..., :NOPE], ((TOK_DEV, 0), (0, 0), (0, 0)))
    values = jnp.pad(key_value[..., NOPE:], ((TOK_DEV, 0), (0, 0), (0, 0)))
    key_rope = jnp.pad(key_rope, ((TOK_DEV, 0), (0, 0)))
    key_docs = jnp.concatenate([jnp.full((TOK_DEV,), -1, jnp.int32), documents.astype(jnp.int32)])
    scale = (NOPE + ROPE) ** (-0.5)

    def one_block(block_index):
        start = (block_index * TOK_DEV).astype(jnp.int32)
        q_nope = lax.dynamic_slice_in_dim(query_nope, start, TOK_DEV, 0).astype(jnp.float32)
        q_rope = lax.dynamic_slice_in_dim(query_rope, start, TOK_DEV, 0).astype(jnp.float32)
        k_nope = lax.dynamic_slice_in_dim(key_nope, start, 2 * TOK_DEV, 0).astype(jnp.float32)
        k_rope = lax.dynamic_slice_in_dim(key_rope, start, 2 * TOK_DEV, 0).astype(jnp.float32)
        v_block = lax.dynamic_slice_in_dim(values, start, 2 * TOK_DEV, 0).astype(jnp.float32)
        q_docs = lax.dynamic_slice_in_dim(documents.astype(jnp.int32), start, TOK_DEV, 0)
        k_docs = lax.dynamic_slice_in_dim(key_docs, start, 2 * TOK_DEV, 0)
        q_pos = start + jnp.arange(TOK_DEV, dtype=jnp.int32)
        k_pos = start - TOK_DEV + jnp.arange(2 * TOK_DEV, dtype=jnp.int32)
        scores = (jnp.einsum('qhd,khd->hqk', q_nope, k_nope) + jnp.einsum('qhr,kr->hqk', q_rope, k_rope)) * scale
        allowed = (k_docs[None, :] == q_docs[:, None]) & (k_pos[None, :] <= q_pos[:, None])
        scores = jnp.where(allowed[None], scores, -1e+30)
        highest = lax.optimization_barrier(jnp.max(scores, axis=-1, keepdims=True))
        weights = jnp.exp(scores - highest)
        probs = (weights / lax.optimization_barrier(jnp.sum(weights, axis=-1, keepdims=True))).astype(jnp.bfloat16)
        attended = jnp.einsum('hqk,khv->qhv', probs.astype(jnp.float32), v_block).astype(jnp.bfloat16)
        return attended.reshape(TOK_DEV, head_count * VDIM)
    attended = lax.map(one_block, jnp.arange(N_CTX, dtype=jnp.int32)).reshape(tokens, N_GRP, HEAD_DEV * VDIM)
    weight_groups = out_weight.reshape(N_GRP, HEAD_DEV * VDIM, D)

    def add_group(running, group):
        rows = lax.dynamic_index_in_dim(attended, group, 1, keepdims=False)
        matrix = lax.dynamic_index_in_dim(weight_groups, group, 0, keepdims=False)
        partial_value = jnp.dot(rows, matrix, preferred_element_type=jnp.float32).astype(jnp.bfloat16)
        partial_value = lax.optimization_barrier(partial_value)
        return (running + partial_value.astype(jnp.float32), None)
    mixed, unused = lax.scan(add_group, jnp.zeros((tokens, D), jnp.float32), jnp.arange(N_GRP, dtype=jnp.int32))
    return mixed.astype(jnp.bfloat16)
```

```python
import jax
import jax.numpy as jnp
from jax import lax
from jax.experimental import pallas as pl
from jax.experimental.pallas import tpu as pltpu
from jax.sharding import PartitionSpec as P

KL = 512
NOPE = 128
ROPE = 64
VDIM = 128
HEAD = NOPE + ROPE
Z = 8
MESH = pl.DeviceIdType.MESH
ANY = pl.BlockSpec(memory_space=pl.ANY)
VM = pl.BlockSpec(memory_space=pltpu.VMEM)
EPSILON = 1e-06


class Place:
    def __init__(self):
        ctx = lax.axis_index("ctx")
        grp = lax.axis_index("grp")
        self.ctx = ctx
        self.z = ctx // 2
        self.y = ctx % 2
        self.chip = grp // 2
        self.core = grp % 2

    def at(self, z=None, y=None, chip=None, core=None):
        z = self.z if z is None else z
        y = self.y if y is None else y
        chip = self.chip if chip is None else chip
        core = self.core if core is None else core
        return (z * 2 + y, chip * 2 + core)


class Sends:
    def __init__(self, send_sems, recv_sems):
        self.send_sems = send_sems
        self.recv_sems = recv_sems
        self.used = 0
        self.started = []

    def slot(self):
        self.used += 1
        return self.used - 1

    def make(self, number, source, target, device):
        return pltpu.make_async_remote_copy(
            source,
            target,
            self.send_sems.at[number],
            self.recv_sems.at[number],
            device_id=device,
            device_id_type=MESH,
        )

    def start(self, number, source, target, device):
        copy = self.make(number, source, target, device)
        copy.start()
        self.started.append(copy)

    def arrived(self, number, target, device):
        self.make(number, target, target, device).wait_recv()

    def drain(self):
        for copy in self.started:
            copy.wait_send()


def enter(devices):
    barrier = pltpu.get_barrier_semaphore()
    for device in devices:
        pl.semaphore_signal(barrier, inc=1, device_id=device, device_id_type=MESH)
    pl.semaphore_wait(barrier, len(devices))


class Ring:
    def __init__(self, sends, place, views):
        self.sends = sends
        self.place = place
        self.views = views
        self.up = place.at(z=(place.z + 1) % Z)
        self.down = place.at(z=(place.z + Z - 1) % Z)
        self.slots = {}

    def number(self, way, steps, part, which):
        key = (way, steps, part, which)
        if key not in self.slots:
            self.slots[key] = self.sends.slot()
        return self.slots[key]

    def reach(self, way, part):
        return 4 if (way == 0) == (part == 0) else 3

    def send(self, way, steps, part, sources):
        if steps > self.reach(way, part):
            return
        origin = (self.place.z + (Z - steps + 1 if way == 0 else steps - 1)) % Z
        targets = self.views(origin, part)
        for which, (source, target) in enumerate(zip(sources or targets, targets)):
            self.sends.start(
                self.number(way, steps, part, which),
                source,
                target,
                self.up if way == 0 else self.down,
            )

    def arrive(self, way, steps, part):
        if steps > self.reach(way, part):
            return
        origin = (self.place.z + (Z - steps if way == 0 else steps)) % Z
        for which, target in enumerate(self.views(origin, part)):
            self.sends.arrived(self.number(way, steps, part, which), target, self.up)
        self.send(way, steps + 1, part, None)


def gather_kernel(
    ql, kvl, qw, kvw, ow, all_ql, all_kvl, all_qw, all_kvw, all_ow, send_sems, recv_sems, local_sems
):
    me = Place()
    peer = me.at(y=1 - me.y)
    twin = me.at(core=1 - me.core)
    above = me.at(z=(me.z + 1) % Z)
    enter([peer, twin, above, me.at(z=(me.z + Z - 1) % Z)])
    sends = Sends(send_sems, recv_sems)

    def views(origin, part):
        row = origin * 2 + (me.y if part == 0 else 1 - me.y)
        return [all_qw.at[row], all_kvw.at[row]]

    def half(array, y):
        width = array.shape[1] // 2
        return array.at[:, pl.ds(pl.multiple_of(y * width, 128), width)]

    ring = Ring(sends, me, views)
    swap_q, swap_kv = sends.slot(), sends.slot()
    sends.start(swap_q, half(qw, 1 - me.y), all_qw.at[me.ctx], peer)
    sends.start(swap_kv, half(kvw, 1 - me.y), all_kvw.at[me.ctx], peer)
    own = [half(qw, me.y), half(kvw, me.y)]
    ring.send(0, 1, 0, own)
    ring.send(1, 1, 0, own)
    local = []
    for number, (source, target) in enumerate(
        [
            (own[0], all_qw.at[me.ctx]),
            (own[1], all_kvw.at[me.ctx]),
            (ql, all_ql.at[me.y]),
            (kvl, all_kvl.at[1 + me.y]),
            (ow, all_ow.at[me.y]),
        ]
    ):
        copy = pltpu.make_async_copy(source, target, local_sems.at[number])
        copy.start()
        local.append(copy)
    rows = ql.shape[0] // 2
    mine = pl.ds(pl.multiple_of(me.core * rows, rows), rows)
    other = pl.ds(pl.multiple_of((1 - me.core) * rows, rows), rows)
    lat_q, lat_kv = sends.slot(), sends.slot()
    sends.start(lat_kv, kvl.at[mine], all_kvl.at[1 + me.y, mine], peer)
    sends.start(lat_q, ql.at[mine], all_ql.at[me.y, mine], peer)
    sends.arrived(swap_q, all_qw.at[me.z * 2 + 1 - me.y], peer)
    sends.arrived(swap_kv, all_kvw.at[me.z * 2 + 1 - me.y], peer)
    ring.send(0, 1, 1, None)
    ring.send(1, 1, 1, None)
    out = sends.slot()
    sends.start(out, ow, all_ow.at[me.y], peer)
    ring.arrive(0, 1, 0)
    ring.arrive(1, 1, 0)
    twin_q, twin_kv, prior, twin_prior = (sends.slot() for _ in range(4))
    local[3].wait()
    sends.arrived(lat_kv, all_kvl.at[2 - me.y, mine], peer)
    sends.start(prior, all_kvl.at[2, mine], all_kvl.at[0, mine], above)
    sends.start(twin_kv, all_kvl.at[2 - me.y, mine], all_kvl.at[2 - me.y, mine], twin)
    ring.arrive(0, 1, 1)
    ring.arrive(1, 1, 1)
    sends.arrived(lat_q, all_ql.at[1 - me.y, mine], peer)
    sends.start(twin_q, all_ql.at[1 - me.y, mine], all_ql.at[1 - me.y, mine], twin)
    ring.arrive(0, 2, 0)
    ring.arrive(1, 2, 0)
    sends.arrived(prior, all_kvl.at[0, mine], above)
    sends.start(twin_prior, all_kvl.at[0, mine], all_kvl.at[0, mine], twin)
    ring.arrive(0, 2, 1)
    ring.arrive(1, 2, 1)
    for part in (0, 1):
        ring.arrive(0, 3, part)
        ring.arrive(1, 3, part)
    ring.arrive(0, 4, 0)
    ring.arrive(1, 4, 1)
    sends.arrived(twin_q, all_ql.at[1 - me.y, other], twin)
    sends.arrived(twin_kv, all_kvl.at[2 - me.y, other], twin)
    sends.arrived(twin_prior, all_kvl.at[0, other], twin)
    sends.arrived(out, all_ow.at[1 - me.y], peer)
    for number in (0, 1, 2, 4):
        local[number].wait()
    sends.drain()


def gather(ql, kvl, qw, kvw, ow):
    rows = ql.shape[0]
    ctx = lax.axis_size("ctx")
    bf16 = jnp.bfloat16
    return pl.pallas_call(
        gather_kernel,
        out_shape=[
            jax.ShapeDtypeStruct((2, rows, ql.shape[1]), bf16),
            jax.ShapeDtypeStruct((3, rows, kvl.shape[1]), bf16),
            jax.ShapeDtypeStruct((ctx, qw.shape[0], qw.shape[1] // 2), bf16),
            jax.ShapeDtypeStruct((ctx, kvw.shape[0], kvw.shape[1] // 2), bf16),
            jax.ShapeDtypeStruct((2, ow.shape[0], ow.shape[1]), bf16),
        ],
        in_specs=[ANY] * 5,
        out_specs=[ANY] * 5,
        scratch_shapes=[
            pltpu.SemaphoreType.DMA((40,)),
            pltpu.SemaphoreType.DMA((40,)),
            pltpu.SemaphoreType.DMA((5,)),
        ],
        compiler_params=pltpu.CompilerParams(collective_id=0, has_side_effects=True),
        name="gather",
    )(ql, kvl, qw, kvw, ow)


def turn(inputs, table):
    half = ROPE // 2
    swapped = jnp.concatenate([inputs[:, half:], inputs[:, :half]], axis=1)
    return inputs * table[:, :ROPE] + swapped * table[:, ROPE:]


def attend_kernel(ql, kvl, qw, kvw, gain, table, query_docs, key_docs, out, query, bias):
    tokens = ql.shape[0]
    rows = tokens // 2
    heads = qw.shape[1] // HEAD
    bf16 = jnp.bfloat16
    latent = kvl[:, :KL].astype(jnp.float32)
    scale = lax.rsqrt(jnp.mean(latent * latent, axis=-1, keepdims=True) + EPSILON)
    normed = (latent * scale * gain[...]).astype(bf16)
    key_rope = turn(kvl[:, KL:].astype(jnp.float32), table[...]).astype(bf16)
    query[...] = jnp.dot(ql[...], qw[...], preferred_element_type=jnp.float32)
    for block in range(2):
        spot_q = lax.broadcasted_iota(jnp.int32, (rows, 2 * rows), 0)
        spot_k = lax.broadcasted_iota(jnp.int32, (rows, 2 * rows), 1)
        same = query_docs[rows * block : rows * (block + 1), :] == key_docs[
            :, rows * block : rows * (block + 2)
        ]
        bias[block] = jnp.where(same & (spot_k - rows <= spot_q), 0.0, -1e30)
    for head in range(heads):
        key_value = jnp.dot(
            normed,
            kvw[:, head * (NOPE + VDIM) : (head + 1) * (NOPE + VDIM)],
            preferred_element_type=jnp.float32,
        ).astype(bf16)
        keys = jnp.concatenate([key_value[:, :NOPE], key_rope], axis=1)
        values = key_value[:, NOPE:]
        nope = query[:, head * HEAD : head * HEAD + NOPE].astype(bf16)
        rope = turn(query[:, head * HEAD + NOPE : (head + 1) * HEAD], table[rows:, :])
        queries = jnp.concatenate([nope, rope.astype(bf16)], axis=1)
        for block in range(2):
            window = slice(rows * block, rows * (block + 2))
            scores = lax.dot_general(
                queries[rows * block : rows * (block + 1)],
                keys[window],
                (((1,), (1,)), ((), ())),
                preferred_element_type=jnp.float32,
            )
            scores = scores * (HEAD ** (-0.5)) + bias[block]
            weights = jnp.exp(scores - jnp.max(scores, axis=-1, keepdims=True))
            total = jnp.sum(weights, axis=-1, keepdims=True)
            mixed = jnp.dot(
                weights.astype(bf16), values[window], preferred_element_type=jnp.float32
            )
            out[block, :, head * VDIM : (head + 1) * VDIM] = (mixed * (1.0 / total)).astype(bf16)


def attend(ql, kvl, qw, kvw, gain, table, query_docs, key_docs):
    tokens = ql.shape[0]
    heads = qw.shape[1] // HEAD
    return pl.pallas_call(
        attend_kernel,
        out_shape=jax.ShapeDtypeStruct((2, tokens // 2, heads * VDIM), jnp.bfloat16),
        in_specs=[VM] * 8,
        out_specs=VM,
        scratch_shapes=[
            pltpu.VMEM((tokens, qw.shape[1]), jnp.float32),
            pltpu.VMEM((2, tokens // 2, tokens), jnp.float32),
        ],
        compiler_params=pltpu.CompilerParams(vmem_limit_bytes=40 << 20),
        name="attend",
    )(ql, kvl, qw, kvw, gain, table, query_docs, key_docs)


def project_kernel(
    att, ow, out, every, kept, given, taken, summed, inbox, final, send_sems, recv_sems, rs_send, rs_recv, last
):
    me = Place()
    peer = me.at(y=1 - me.y)
    twin = me.at(core=1 - me.core)
    above = me.at(z=(me.z + 1) % Z)
    below = me.at(z=(me.z + Z - 1) % Z)
    goal_z = (me.chip + 4) % Z
    goal = me.at(z=goal_z, chip=me.z)
    origin = me.at(z=me.chip, chip=(me.z + 4) % Z)
    fellows = [me.at(chip=(me.chip + step) % Z) for step in range(1, Z)]
    enter([peer, twin, above, below, goal, origin] + fellows)
    sends = Sends(send_sems, recv_sems)
    depth = att.shape[2]

    def views(z, part):
        return [every.at[z, me.y if part == 0 else 1 - me.y]]

    ring = Ring(sends, me, views)
    swap = sends.slot()
    sends.start(swap, att.at[1 - me.y], every.at[me.z, me.y], peer)
    own = [att.at[me.y]]
    ring.send(0, 1, 0, own)
    ring.send(1, 1, 0, own)
    twins = [sends.slot() for _ in range(Z)]

    def product(first, second, which):
        rows = pl.ds(pl.multiple_of(me.y * depth, depth), depth)
        others = pl.ds(pl.multiple_of((1 - me.y) * depth, depth), depth)
        return jnp.dot(
            first, ow[which, rows, :], preferred_element_type=jnp.float32
        ) + jnp.dot(second, ow[which, others, :], preferred_element_type=jnp.float32)

    def tile(number, z):
        first = att[me.y] if number == 0 else every[z, me.y]
        second = every[z, 1 - me.y]
        given[number] = product(first, second, 1 - me.core).astype(jnp.bfloat16)
        sends.start(twins[number], given.at[number], taken.at[number], twin)
        kept[number % 2] = product(first, second, me.core)

    def reduce_to(number, z, start):
        target = (z + 4) % Z
        copy = pltpu.make_async_remote_copy(
            summed.at[number],
            inbox.at[me.chip],
            rs_send.at[number],
            rs_recv.at[me.chip],
            device_id=me.at(chip=target),
            device_id_type=MESH,
        )

        @pl.when(target != me.chip)
        def _():
            if start:
                copy.start()
            else:
                copy.wait_send()

        if start:

            @pl.when(target == me.chip)
            def _():
                inbox[target] = summed[number]

    def hand_over(number, z):
        sends.arrived(twins[number], taken.at[number], twin)
        summed[number] = (kept[number % 2] + taken[number].astype(jnp.float32)).astype(jnp.bfloat16)
        reduce_to(number, z, True)

    offsets = [0, 7, 1, 6, 2, 5, 3, 4]
    blocks = [(me.z + offset) % Z for offset in offsets]
    sends.arrived(swap, every.at[me.z, 1 - me.y], peer)
    ring.send(0, 1, 1, None)
    ring.send(1, 1, 1, None)
    tile(0, blocks[0])
    for steps in range(1, 4):
        for part in (0, 1):
            ring.arrive(0, steps, part)
            ring.arrive(1, steps, part)
        for number in (2 * steps - 1, 2 * steps):
            hand_over(number - 1, blocks[number - 1])
            tile(number, blocks[number])
    ring.arrive(0, 4, 0)
    ring.arrive(1, 4, 1)
    hand_over(6, blocks[6])
    tile(7, blocks[7])
    hand_over(7, blocks[7])
    for step in range(1, Z):
        source = (me.chip + step) % Z
        pltpu.make_async_remote_copy(
            inbox.at[source],
            inbox.at[source],
            rs_send.at[0],
            rs_recv.at[source],
            device_id=me.at(chip=source),
            device_id_type=MESH,
        ).wait_recv()
    total = inbox[0].astype(jnp.float32)
    for source in range(1, Z):
        total = total + inbox[source].astype(jnp.float32)
    final[0] = total.astype(jnp.bfloat16)
    move = pltpu.make_async_remote_copy(
        final.at[0], final.at[1], last.at[0], last.at[1], device_id=goal, device_id_type=MESH
    )
    move.start()
    for number in range(Z):
        reduce_to(number, blocks[number], False)
    sends.drain()
    move.wait()
    out[...] = final[1]


def project(att, ow):
    _, rows, depth = att.shape
    columns = ow.shape[2]
    bf16 = jnp.bfloat16
    return pl.pallas_call(
        project_kernel,
        out_shape=jax.ShapeDtypeStruct((rows, columns), bf16),
        in_specs=[VM] * 2,
        out_specs=VM,
        scratch_shapes=[
            pltpu.VMEM((Z, 2, rows, depth), bf16),
            pltpu.VMEM((2, rows, columns), jnp.float32),
            pltpu.VMEM((Z, rows, columns), bf16),
            pltpu.VMEM((Z, rows, columns), bf16),
            pltpu.VMEM((Z, rows, columns), bf16),
            pltpu.VMEM((Z, rows, columns), bf16),
            pltpu.VMEM((2, rows, columns), bf16),
            pltpu.SemaphoreType.DMA((32,)),
            pltpu.SemaphoreType.DMA((32,)),
            pltpu.SemaphoreType.DMA((Z,)),
            pltpu.SemaphoreType.DMA((Z,)),
            pltpu.SemaphoreType.DMA((2,)),
        ],
        compiler_params=pltpu.CompilerParams(
            collective_id=1, has_side_effects=True, vmem_limit_bytes=40 << 20
        ),
        name="project",
    )(att, ow)


def per_device(q_latent, kv_latent, kv_gain, q_weight, kv_weight, out_weight, documents):
    rows = q_latent.shape[0]
    z = lax.axis_index("ctx") // 2
    ql, kvl, qw, kvw, ow = gather(q_latent, kv_latent, q_weight, kv_weight, out_weight)
    positions = z * 2 * rows - rows + jnp.arange(3 * rows, dtype=jnp.int32)
    inverse = 10000.0 ** (-2.0 * jnp.arange(ROPE // 2, dtype=jnp.float32) / ROPE)
    angles = positions.astype(jnp.float32)[:, None] * inverse[None, :]
    cosine, sine = jnp.cos(angles), jnp.sin(angles)
    table = jnp.concatenate([cosine, cosine, -sine, sine], axis=1)
    padded = jnp.concatenate([jnp.full((rows,), -1, jnp.int32), documents])
    key_docs = lax.dynamic_slice_in_dim(padded, z * 2 * rows, 3 * rows, 0)
    att = attend(
        ql.reshape(2 * rows, -1),
        kvl.reshape(3 * rows, -1),
        qw.reshape(-1, qw.shape[2]),
        kvw.reshape(-1, kvw.shape[2]),
        kv_gain[None, :],
        table,
        key_docs[rows:, None],
        key_docs[None, :],
    )
    return project(att, ow)


def solution(mesh):
    return jax.shard_map(
        per_device,
        mesh=mesh,
        in_specs=(
            P("ctx", None),
            P("ctx", None),
            P(),
            P("ctx", "grp"),
            P("ctx", "grp"),
            P("grp", "ctx"),
            P(),
        ),
        out_specs=P("ctx", "grp"),
        check_vma=False,
    )
```

```python
import jax
import jax.numpy as jnp
from jax import lax
from jax.experimental import pallas as pl
from jax.experimental.pallas import tpu as pltpu
from jax.sharding import PartitionSpec as P

KL = 512
NOPE = 128
ROPE = 64
VDIM = 128
HEAD = NOPE + ROPE
Z = 8
MESH = pl.DeviceIdType.MESH
VM = pl.BlockSpec(memory_space=pltpu.VMEM)
EPSILON = 1e-06


OFFSETS = [0, 7, 1, 6, 2, 5, 3, 4]
REDUCERS = [(1, 2), (1, 3), (1, 1), (0, 2), (1, 0), (0, 3), (0, 1), (0, 0)]


def reducer(number, z):
    row, column = REDUCERS[number]
    return (z // 4 + row) % 2 * 4 + (z + column) % 4


def choose(pick, first, second):
    return tuple(jnp.where(pick, a, b) for a, b in zip(first, second))


class Place:
    def __init__(self):
        ctx = lax.axis_index("ctx")
        grp = lax.axis_index("grp")
        self.ctx = ctx
        self.z = ctx // 2
        self.y = ctx % 2
        self.chip = grp // 2
        self.core = grp % 2

    def at(self, z=None, y=None, chip=None, core=None):
        z = self.z if z is None else z
        y = self.y if y is None else y
        chip = self.chip if chip is None else chip
        core = self.core if core is None else core
        return (z * 2 + y, chip * 2 + core)


class Sends:
    def __init__(self, send_sems, recv_sems):
        self.send_sems = send_sems
        self.recv_sems = recv_sems
        self.used = 0
        self.started = []

    def slot(self):
        self.used += 1
        return self.used - 1

    def make(self, number, source, target, device):
        return pltpu.make_async_remote_copy(
            source,
            target,
            self.send_sems.at[number],
            self.recv_sems.at[number],
            device_id=device,
            device_id_type=MESH,
        )

    def start(self, number, source, target, device):
        copy = self.make(number, source, target, device)
        copy.start()
        self.started.append(copy)

    def arrived(self, number, target, device):
        self.make(number, target, target, device).wait_recv()

    def drain(self):
        for copy in self.started:
            copy.wait_send()


def enter(devices):
    barrier = pltpu.get_barrier_semaphore()
    for device in devices:
        pl.semaphore_signal(barrier, inc=1, device_id=device, device_id_type=MESH)
    pl.semaphore_wait(barrier, len(devices))


class Ring:
    def __init__(self, sends, place, views):
        self.sends = sends
        self.place = place
        self.views = views
        self.up = place.at(z=(place.z + 1) % Z)
        self.down = place.at(z=(place.z + Z - 1) % Z)
        self.slots = {}

    def number(self, way, steps, part, which):
        key = (way, steps, part, which)
        if key not in self.slots:
            self.slots[key] = self.sends.slot()
        return self.slots[key]

    def reach(self, way, part):
        return 4 if (way == 0) == (part == 0) else 3

    def send(self, way, steps, part, sources):
        if steps > self.reach(way, part):
            return
        origin = (self.place.z + (Z - steps + 1 if way == 0 else steps - 1)) % Z
        targets = self.views(origin, part)
        for which, (source, target) in enumerate(zip(sources or targets, targets)):
            self.sends.start(
                self.number(way, steps, part, which),
                source,
                target,
                self.up if way == 0 else self.down,
            )

    def arrive(self, way, steps, part):
        if steps > self.reach(way, part):
            return
        origin = (self.place.z + (Z - steps if way == 0 else steps)) % Z
        for which, target in enumerate(self.views(origin, part)):
            self.sends.arrived(self.number(way, steps, part, which), target, self.up)
        self.send(way, steps + 1, part, None)


def gather_kernel(
    ql, kvl, qw, kvw, ow, all_ql, all_kvl, all_qw, all_kvw, all_ow, send_sems, recv_sems, local_sems
):
    me = Place()
    peer = me.at(y=1 - me.y)
    twin = me.at(core=1 - me.core)
    above = me.at(z=(me.z + 1) % Z)
    enter([peer, twin, above, me.at(z=(me.z + Z - 1) % Z)])
    sends = Sends(send_sems, recv_sems)

    def views(origin, part):
        row = origin * 2 + (me.y if part == 0 else 1 - me.y)
        return [all_qw.at[row], all_kvw.at[row]]

    def half(array, y):
        width = array.shape[1] // 2
        return array.at[:, pl.ds(pl.multiple_of(y * width, 128), width)]

    ring = Ring(sends, me, views)
    swap_q, swap_kv = sends.slot(), sends.slot()
    sends.start(swap_q, half(qw, 1 - me.y), all_qw.at[me.ctx], peer)
    sends.start(swap_kv, half(kvw, 1 - me.y), all_kvw.at[me.ctx], peer)
    own = [half(qw, me.y), half(kvw, me.y)]
    ring.send(0, 1, 0, own)
    ring.send(1, 1, 0, own)
    local = []
    for number, (source, target) in enumerate(
        [
            (own[0], all_qw.at[me.ctx]),
            (own[1], all_kvw.at[me.ctx]),
            (ql, all_ql.at[me.y]),
            (kvl, all_kvl.at[1 + me.y]),
            (ow, all_ow.at[me.y]),
        ]
    ):
        copy = pltpu.make_async_copy(source, target, local_sems.at[number])
        copy.start()
        local.append(copy)
    rows = ql.shape[0] // 2
    mine = pl.ds(pl.multiple_of(me.core * rows, rows), rows)
    other = pl.ds(pl.multiple_of((1 - me.core) * rows, rows), rows)
    lat_q, lat_kv = sends.slot(), sends.slot()
    sends.start(lat_kv, kvl.at[:, mine], all_kvl.at[1 + me.y, :, mine], peer)
    sends.start(lat_q, ql.at[mine], all_ql.at[me.y, mine], peer)
    sends.arrived(swap_q, all_qw.at[me.z * 2 + 1 - me.y], peer)
    sends.arrived(swap_kv, all_kvw.at[me.z * 2 + 1 - me.y], peer)
    ring.send(0, 1, 1, None)
    ring.send(1, 1, 1, None)
    out = sends.slot()
    sends.start(out, ow, all_ow.at[me.y], peer)
    ring.arrive(0, 1, 0)
    ring.arrive(1, 1, 0)
    twin_q, twin_kv, prior, twin_prior = (sends.slot() for _ in range(4))
    local[3].wait()
    sends.arrived(lat_kv, all_kvl.at[2 - me.y, :, mine], peer)
    sends.start(prior, all_kvl.at[2, :, mine], all_kvl.at[0, :, mine], above)
    sends.start(
        twin_kv, all_kvl.at[2 - me.y, :, mine], all_kvl.at[2 - me.y, :, mine], twin
    )
    ring.arrive(0, 1, 1)
    ring.arrive(1, 1, 1)
    sends.arrived(lat_q, all_ql.at[1 - me.y, mine], peer)
    sends.start(twin_q, all_ql.at[1 - me.y, mine], all_ql.at[1 - me.y, mine], twin)
    ring.arrive(0, 2, 0)
    ring.arrive(1, 2, 0)
    sends.arrived(prior, all_kvl.at[0, :, mine], above)
    sends.start(twin_prior, all_kvl.at[0, :, mine], all_kvl.at[0, :, mine], twin)
    ring.arrive(0, 2, 1)
    ring.arrive(1, 2, 1)
    for part in (0, 1):
        ring.arrive(0, 3, part)
        ring.arrive(1, 3, part)
    ring.arrive(0, 4, 0)
    ring.arrive(1, 4, 1)
    sends.arrived(twin_q, all_ql.at[1 - me.y, other], twin)
    sends.arrived(twin_kv, all_kvl.at[2 - me.y, :, other], twin)
    sends.arrived(twin_prior, all_kvl.at[0, :, other], twin)
    sends.arrived(out, all_ow.at[1 - me.y], peer)
    for number in (0, 1, 2, 4):
        local[number].wait()
    sends.drain()


def gather(ql, kvl, qw, kvw, ow):
    rows = ql.shape[0]
    ctx = lax.axis_size("ctx")
    bf16 = jnp.bfloat16
    return pl.pallas_call(
        gather_kernel,
        out_shape=[
            jax.ShapeDtypeStruct((2, rows, ql.shape[1]), bf16),
            jax.ShapeDtypeStruct((3, kvl.shape[0], rows), bf16),
            jax.ShapeDtypeStruct((ctx, qw.shape[0], qw.shape[1] // 2), bf16),
            jax.ShapeDtypeStruct((ctx, kvw.shape[0], kvw.shape[1] // 2), bf16),
            jax.ShapeDtypeStruct((2, ow.shape[0], ow.shape[1]), bf16),
        ],
        in_specs=[VM] * 5,
        out_specs=[VM] * 5,
        scratch_shapes=[
            pltpu.SemaphoreType.DMA((40,)),
            pltpu.SemaphoreType.DMA((40,)),
            pltpu.SemaphoreType.DMA((5,)),
        ],
        compiler_params=pltpu.CompilerParams(
            collective_id=0, has_side_effects=True, vmem_limit_bytes=40 << 20
        ),
        name="gather",
    )(ql, kvl, qw, kvw, ow)


def dot_transposed(left, right):
    return lax.dot_general(
        left, right, (((1,), (1,)), ((), ())), preferred_element_type=jnp.float32
    )


def turn(inputs, table):
    half = ROPE // 2
    swapped = jnp.concatenate([inputs[:, half:], inputs[:, :half]], axis=1)
    return inputs * table[:, :ROPE] + swapped * table[:, ROPE:]


def attend_kernel(ql, kvl, qw, kvw, gain, table, query_docs, key_docs, out, query, bias):
    tokens = ql.shape[0]
    rows = tokens // 2
    heads = qw.shape[1] // HEAD
    bf16 = jnp.bfloat16
    latents = jnp.concatenate([kvl[number].astype(jnp.float32).T for number in range(3)], axis=0)
    latent = latents[:, :KL]
    scale = lax.rsqrt(jnp.mean(latent * latent, axis=-1, keepdims=True) + EPSILON)
    normed = (latent * scale * gain[...]).astype(bf16)
    key_rope = turn(latents[:, KL:], table[...]).astype(bf16)
    query[...] = jnp.dot(ql[...], qw[...], preferred_element_type=jnp.float32)
    for block in range(2):
        spot_q = lax.broadcasted_iota(jnp.int32, (rows, 2 * rows), 0)
        spot_k = lax.broadcasted_iota(jnp.int32, (rows, 2 * rows), 1)
        same = query_docs[rows * block : rows * (block + 1), :] == key_docs[
            :, rows * block : rows * (block + 2)
        ]
        bias[block] = jnp.where(same & (spot_k - rows <= spot_q), 0.0, -1e30)
    for head in range(heads):
        key_value = jnp.dot(
            normed,
            kvw[:, head * (NOPE + VDIM) : (head + 1) * (NOPE + VDIM)],
            preferred_element_type=jnp.float32,
        ).astype(bf16)
        keys = jnp.concatenate([key_value[:, :NOPE], key_rope], axis=1)
        values = key_value[:, NOPE:]
        nope = query[:, head * HEAD : head * HEAD + NOPE].astype(bf16)
        rope = turn(query[:, head * HEAD + NOPE : (head + 1) * HEAD], table[rows:, :])
        queries = jnp.concatenate([nope, rope.astype(bf16)], axis=1)
        for block in range(2):
            window = slice(rows * block, rows * (block + 2))
            scores = dot_transposed(queries[rows * block : rows * (block + 1)], keys[window])
            scores = scores * (HEAD ** (-0.5)) + bias[block]
            weights = jnp.exp(scores - jnp.max(scores, axis=-1, keepdims=True))
            total = jnp.sum(weights, axis=-1, keepdims=True)
            mixed = jnp.dot(
                weights.astype(bf16), values[window], preferred_element_type=jnp.float32
            )
            out[block, :, head * VDIM : (head + 1) * VDIM] = (mixed * (1.0 / total)).astype(bf16)


def attend(ql, kvl, qw, kvw, gain, table, query_docs, key_docs):
    tokens = ql.shape[0]
    heads = qw.shape[1] // HEAD
    return pl.pallas_call(
        attend_kernel,
        out_shape=jax.ShapeDtypeStruct((2, tokens // 2, heads * VDIM), jnp.bfloat16),
        in_specs=[VM] * 8,
        out_specs=VM,
        scratch_shapes=[
            pltpu.VMEM((tokens, qw.shape[1]), jnp.float32),
            pltpu.VMEM((2, tokens // 2, tokens), jnp.float32),
        ],
        compiler_params=pltpu.CompilerParams(vmem_limit_bytes=40 << 20),
        name="attend",
    )(ql, kvl, qw, kvw, gain, table, query_docs, key_docs)


def project_kernel(
    att, ow, out, every, kept, given, taken, summed, inbox, final, send_sems, recv_sems, rs_send, rs_recv, last
):
    me = Place()
    peer = me.at(y=1 - me.y)
    twin = me.at(core=1 - me.core)
    above = me.at(z=(me.z + 1) % Z)
    below = me.at(z=(me.z + Z - 1) % Z)
    goal, origin = twin, twin
    for number, offset in enumerate(OFFSETS):
        pick = reducer(number, me.z) == me.chip
        goal = choose(pick, me.at(z=(me.z + offset) % Z, chip=me.z), goal)
        pick = (me.z - me.chip + Z) % Z == offset
        origin = choose(pick, me.at(z=me.chip, chip=reducer(number, me.chip)), origin)
    fellows = [me.at(chip=(me.chip + step) % Z) for step in range(1, Z)]
    enter([peer, twin, above, below, goal, origin] + fellows)
    sends = Sends(send_sems, recv_sems)
    depth = att.shape[2]

    def views(z, part):
        return [every.at[z, me.y if part == 0 else 1 - me.y]]

    ring = Ring(sends, me, views)
    swap = sends.slot()
    sends.start(swap, att.at[1 - me.y], every.at[me.z, me.y], peer)
    own = [att.at[me.y]]
    ring.send(0, 1, 0, own)
    ring.send(1, 1, 0, own)
    twins = [sends.slot() for _ in range(Z)]

    def product(first, second, which):
        rows = pl.ds(pl.multiple_of(me.y * depth, depth), depth)
        others = pl.ds(pl.multiple_of((1 - me.y) * depth, depth), depth)
        return dot_transposed(first, ow[which, :, rows]) + dot_transposed(
            second, ow[which, :, others]
        )

    def tile(number, z):
        first = att[me.y] if number == 0 else every[z, me.y]
        second = every[z, 1 - me.y]
        given[number] = product(first, second, 1 - me.core).astype(jnp.bfloat16)
        sends.start(twins[number], given.at[number], taken.at[number], twin)
        kept[number % 2] = product(first, second, me.core)

    def reduce_to(number, start):
        target = reducer(number, me.z)
        copy = pltpu.make_async_remote_copy(
            summed.at[number],
            inbox.at[me.chip],
            rs_send.at[number],
            rs_recv.at[me.chip],
            device_id=me.at(chip=target),
            device_id_type=MESH,
        )

        @pl.when(target != me.chip)
        def _():
            if start:
                copy.start()
            else:
                copy.wait_send()

        if start:

            @pl.when(target == me.chip)
            def _():
                inbox[target] = summed[number]

    def hand_over(number):
        sends.arrived(twins[number], taken.at[number], twin)
        summed[number] = (kept[number % 2] + taken[number].astype(jnp.float32)).astype(jnp.bfloat16)
        reduce_to(number, True)

    move = pltpu.make_async_remote_copy(
        final.at[0], final.at[1], last.at[0], last.at[1], device_id=goal, device_id_type=MESH
    )

    def finish(number):
        @pl.when(reducer(number, me.z) == me.chip)
        def _():
            for step in range(1, Z):
                source = (me.chip + step) % Z
                pltpu.make_async_remote_copy(
                    inbox.at[source],
                    inbox.at[source],
                    rs_send.at[0],
                    rs_recv.at[source],
                    device_id=me.at(chip=source),
                    device_id_type=MESH,
                ).wait_recv()
            total = inbox[0].astype(jnp.float32)
            for source in range(1, Z):
                total = total + inbox[source].astype(jnp.float32)
            final[0] = total.astype(jnp.bfloat16)
            move.start()

    blocks = [(me.z + offset) % Z for offset in OFFSETS]
    sends.arrived(swap, every.at[me.z, 1 - me.y], peer)
    ring.send(0, 1, 1, None)
    ring.send(1, 1, 1, None)
    tile(0, blocks[0])
    for steps in range(1, 4):
        for part in (0, 1):
            ring.arrive(0, steps, part)
            ring.arrive(1, steps, part)
        for number in (2 * steps - 1, 2 * steps):
            hand_over(number - 1)
            tile(number, blocks[number])
            if number >= 3:
                finish(number - 3)
    ring.arrive(0, 4, 0)
    ring.arrive(1, 4, 1)
    hand_over(6)
    tile(7, blocks[7])
    hand_over(7)
    for number in range(4, Z):
        finish(number)
    for number in range(Z):
        reduce_to(number, False)
    sends.drain()
    move.wait()
    out[...] = final[1]


def project(att, ow):
    _, rows, depth = att.shape
    columns = ow.shape[1]
    bf16 = jnp.bfloat16
    return pl.pallas_call(
        project_kernel,
        out_shape=jax.ShapeDtypeStruct((rows, columns), bf16),
        in_specs=[VM] * 2,
        out_specs=VM,
        scratch_shapes=[
            pltpu.VMEM((Z, 2, rows, depth), bf16),
            pltpu.VMEM((2, rows, columns), jnp.float32),
            pltpu.VMEM((Z, rows, columns), bf16),
            pltpu.VMEM((Z, rows, columns), bf16),
            pltpu.VMEM((Z, rows, columns), bf16),
            pltpu.VMEM((Z, rows, columns), bf16),
            pltpu.VMEM((2, rows, columns), bf16),
            pltpu.SemaphoreType.DMA((32,)),
            pltpu.SemaphoreType.DMA((32,)),
            pltpu.SemaphoreType.DMA((Z,)),
            pltpu.SemaphoreType.DMA((Z,)),
            pltpu.SemaphoreType.DMA((2,)),
        ],
        compiler_params=pltpu.CompilerParams(
            collective_id=1, has_side_effects=True, vmem_limit_bytes=40 << 20
        ),
        name="project",
    )(att, ow)


def per_device(q_latent, kv_latent, kv_gain, q_weight, kv_weight, out_weight, documents):
    rows = q_latent.shape[0]
    z = lax.axis_index("ctx") // 2
    ql, kvl, qw, kvw, ow = gather(q_latent, kv_latent.T, q_weight, kv_weight, out_weight.T)
    positions = z * 2 * rows - rows + jnp.arange(3 * rows, dtype=jnp.int32)
    inverse = 10000.0 ** (-2.0 * jnp.arange(ROPE // 2, dtype=jnp.float32) / ROPE)
    angles = positions.astype(jnp.float32)[:, None] * inverse[None, :]
    cosine, sine = jnp.cos(angles), jnp.sin(angles)
    table = jnp.concatenate([cosine, cosine, -sine, sine], axis=1)
    padded = jnp.concatenate([jnp.full((rows,), -1, jnp.int32), documents])
    key_docs = lax.dynamic_slice_in_dim(padded, z * 2 * rows, 3 * rows, 0)
    att = attend(
        ql.reshape(2 * rows, -1),
        kvl,
        qw.reshape(-1, qw.shape[2]),
        kvw.reshape(-1, kvw.shape[2]),
        kv_gain[None, :],
        table,
        key_docs[rows:, None],
        key_docs[None, :],
    )
    return project(att, ow)


def solution(mesh):
    return jax.shard_map(
        per_device,
        mesh=mesh,
        in_specs=(
            P("ctx", None),
            P("ctx", None),
            P(),
            P("ctx", "grp"),
            P("ctx", "grp"),
            P("grp", "ctx"),
            P(),
        ),
        out_specs=P("ctx", "grp"),
        check_vma=False,
    )
```

```python
import jax
import jax.numpy as jnp
from jax import lax
from jax.experimental import pallas as pl
from jax.experimental.pallas import tpu as pltpu
from jax.sharding import PartitionSpec as P

KL = 512
NOPE = 128
ROPE = 64
VDIM = 128
HEAD = NOPE + ROPE
Z = 8
MESH = pl.DeviceIdType.MESH
VM = pl.BlockSpec(memory_space=pltpu.VMEM)
EPSILON = 1e-06


OFFSETS = [0, 7, 1, 6, 2, 5, 3, 4]


class Place:
    def __init__(self):
        ctx = lax.axis_index("ctx")
        grp = lax.axis_index("grp")
        self.ctx = ctx
        self.z = ctx // 2
        self.y = ctx % 2
        self.chip = grp // 2
        self.core = grp % 2

    def at(self, z=None, y=None, chip=None, core=None):
        z = self.z if z is None else z
        y = self.y if y is None else y
        chip = self.chip if chip is None else chip
        core = self.core if core is None else core
        return (z * 2 + y, chip * 2 + core)


class Sends:
    def __init__(self, send_sems, recv_sems):
        self.send_sems = send_sems
        self.recv_sems = recv_sems
        self.used = 0
        self.started = []

    def slot(self):
        self.used += 1
        return self.used - 1

    def make(self, number, source, target, device):
        return pltpu.make_async_remote_copy(
            source,
            target,
            self.send_sems.at[number],
            self.recv_sems.at[number],
            device_id=device,
            device_id_type=MESH,
        )

    def start(self, number, source, target, device):
        copy = self.make(number, source, target, device)
        copy.start()
        self.started.append(copy)

    def arrived(self, number, target, device):
        self.make(number, target, target, device).wait_recv()

    def drain(self):
        for copy in self.started:
            copy.wait_send()


def enter(devices):
    barrier = pltpu.get_barrier_semaphore()
    for device in devices:
        pl.semaphore_signal(barrier, inc=1, device_id=device, device_id_type=MESH)
    pl.semaphore_wait(barrier, len(devices))


class Ring:
    def __init__(self, sends, place, views):
        self.sends = sends
        self.place = place
        self.views = views
        self.up = place.at(z=(place.z + 1) % Z)
        self.down = place.at(z=(place.z + Z - 1) % Z)
        self.slots = {}

    def number(self, way, steps, part, which):
        key = (way, steps, part, which)
        if key not in self.slots:
            self.slots[key] = self.sends.slot()
        return self.slots[key]

    def reach(self, way, part):
        return 4 if (way == 0) == (part == 0) else 3

    def send(self, way, steps, part, sources):
        if steps > self.reach(way, part):
            return
        origin = (self.place.z + (Z - steps + 1 if way == 0 else steps - 1)) % Z
        targets = self.views(origin, part)
        for which, (source, target) in enumerate(zip(sources or targets, targets)):
            self.sends.start(
                self.number(way, steps, part, which),
                source,
                target,
                self.up if way == 0 else self.down,
            )

    def arrive(self, way, steps, part):
        if steps > self.reach(way, part):
            return
        origin = (self.place.z + (Z - steps if way == 0 else steps)) % Z
        for which, target in enumerate(self.views(origin, part)):
            self.sends.arrived(self.number(way, steps, part, which), target, self.up)
        self.send(way, steps + 1, part, None)


def gather_kernel(
    ql, kvl, qw, kvw, ow, all_ql, all_kvl, all_qw, all_kvw, all_ow, send_sems, recv_sems, local_sems
):
    me = Place()
    peer = me.at(y=1 - me.y)
    twin = me.at(core=1 - me.core)
    above = me.at(z=(me.z + 1) % Z)
    enter([peer, twin, above, me.at(z=(me.z + Z - 1) % Z)])
    sends = Sends(send_sems, recv_sems)

    def views(origin, part):
        row = origin * 2 + (me.y if part == 0 else 1 - me.y)
        return [all_qw.at[row], all_kvw.at[row]]

    def half(array, y):
        width = array.shape[1] // 2
        return array.at[:, pl.ds(pl.multiple_of(y * width, 128), width)]

    ring = Ring(sends, me, views)
    swap_q, swap_kv = sends.slot(), sends.slot()
    sends.start(swap_q, half(qw, 1 - me.y), all_qw.at[me.ctx], peer)
    sends.start(swap_kv, half(kvw, 1 - me.y), all_kvw.at[me.ctx], peer)
    own = [half(qw, me.y), half(kvw, me.y)]
    ring.send(0, 1, 0, own)
    ring.send(1, 1, 0, own)
    local = []
    for number, (source, target) in enumerate(
        [
            (own[0], all_qw.at[me.ctx]),
            (own[1], all_kvw.at[me.ctx]),
            (ql, all_ql.at[me.y]),
            (kvl, all_kvl.at[1 + me.y]),
            (ow, all_ow.at[me.y]),
        ]
    ):
        copy = pltpu.make_async_copy(source, target, local_sems.at[number])
        copy.start()
        local.append(copy)
    rows = ql.shape[0] // 2
    mine = pl.ds(pl.multiple_of(me.core * rows, rows), rows)
    other = pl.ds(pl.multiple_of((1 - me.core) * rows, rows), rows)
    lat_q, lat_kv = sends.slot(), sends.slot()
    sends.start(lat_kv, kvl.at[:, mine], all_kvl.at[1 + me.y, :, mine], peer)
    sends.start(lat_q, ql.at[mine], all_ql.at[me.y, mine], peer)
    sends.arrived(swap_q, all_qw.at[me.z * 2 + 1 - me.y], peer)
    sends.arrived(swap_kv, all_kvw.at[me.z * 2 + 1 - me.y], peer)
    ring.send(0, 1, 1, None)
    ring.send(1, 1, 1, None)
    out = sends.slot()
    sends.start(out, ow, all_ow.at[me.y], peer)
    ring.arrive(0, 1, 0)
    ring.arrive(1, 1, 0)
    twin_q, twin_kv, prior, twin_prior = (sends.slot() for _ in range(4))
    local[3].wait()
    sends.arrived(lat_kv, all_kvl.at[2 - me.y, :, mine], peer)
    sends.start(prior, all_kvl.at[2, :, mine], all_kvl.at[0, :, mine], above)
    sends.start(
        twin_kv, all_kvl.at[2 - me.y, :, mine], all_kvl.at[2 - me.y, :, mine], twin
    )
    ring.arrive(0, 1, 1)
    ring.arrive(1, 1, 1)
    sends.arrived(lat_q, all_ql.at[1 - me.y, mine], peer)
    sends.start(twin_q, all_ql.at[1 - me.y, mine], all_ql.at[1 - me.y, mine], twin)
    ring.arrive(0, 2, 0)
    ring.arrive(1, 2, 0)
    sends.arrived(prior, all_kvl.at[0, :, mine], above)
    sends.start(twin_prior, all_kvl.at[0, :, mine], all_kvl.at[0, :, mine], twin)
    ring.arrive(0, 2, 1)
    ring.arrive(1, 2, 1)
    for part in (0, 1):
        ring.arrive(0, 3, part)
        ring.arrive(1, 3, part)
    ring.arrive(0, 4, 0)
    ring.arrive(1, 4, 1)
    sends.arrived(twin_q, all_ql.at[1 - me.y, other], twin)
    sends.arrived(twin_kv, all_kvl.at[2 - me.y, :, other], twin)
    sends.arrived(twin_prior, all_kvl.at[0, :, other], twin)
    sends.arrived(out, all_ow.at[1 - me.y], peer)
    for number in (0, 1, 2, 4):
        local[number].wait()
    sends.drain()


def gather(ql, kvl, qw, kvw, ow):
    rows = ql.shape[0]
    ctx = lax.axis_size("ctx")
    bf16 = jnp.bfloat16
    return pl.pallas_call(
        gather_kernel,
        out_shape=[
            jax.ShapeDtypeStruct((2, rows, ql.shape[1]), bf16),
            jax.ShapeDtypeStruct((3, kvl.shape[0], rows), bf16),
            jax.ShapeDtypeStruct((ctx, qw.shape[0], qw.shape[1] // 2), bf16),
            jax.ShapeDtypeStruct((ctx, kvw.shape[0], kvw.shape[1] // 2), bf16),
            jax.ShapeDtypeStruct((2, ow.shape[0], ow.shape[1]), bf16),
        ],
        in_specs=[VM] * 5,
        out_specs=[VM] * 5,
        scratch_shapes=[
            pltpu.SemaphoreType.DMA((40,)),
            pltpu.SemaphoreType.DMA((40,)),
            pltpu.SemaphoreType.DMA((5,)),
        ],
        compiler_params=pltpu.CompilerParams(
            collective_id=0, has_side_effects=True, vmem_limit_bytes=40 << 20
        ),
        name="gather",
    )(ql, kvl, qw, kvw, ow)


def dot_transposed(left, right):
    return lax.dot_general(
        left, right, (((1,), (1,)), ((), ())), preferred_element_type=jnp.float32
    )


def turn(inputs, table):
    half = ROPE // 2
    swapped = jnp.concatenate([inputs[:, half:], inputs[:, :half]], axis=1)
    return inputs * table[:, :ROPE] + swapped * table[:, ROPE:]


def attend_kernel(ql, kvl, qw, kvw, gain, table, query_docs, key_docs, out, query, bias):
    tokens = ql.shape[0]
    rows = tokens // 2
    heads = qw.shape[1] // HEAD
    bf16 = jnp.bfloat16
    latents = jnp.concatenate([kvl[number].astype(jnp.float32).T for number in range(3)], axis=0)
    latent = latents[:, :KL]
    scale = lax.rsqrt(jnp.mean(latent * latent, axis=-1, keepdims=True) + EPSILON)
    normed = (latent * scale * gain[...]).astype(bf16)
    key_rope = turn(latents[:, KL:], table[...]).astype(bf16)
    query[...] = jnp.dot(ql[...], qw[...], preferred_element_type=jnp.float32)
    for block in range(2):
        spot_q = lax.broadcasted_iota(jnp.int32, (rows, 2 * rows), 0)
        spot_k = lax.broadcasted_iota(jnp.int32, (rows, 2 * rows), 1)
        same = query_docs[rows * block : rows * (block + 1), :] == key_docs[
            :, rows * block : rows * (block + 2)
        ]
        bias[block] = jnp.where(same & (spot_k - rows <= spot_q), 0.0, -1e30)
    for head in range(heads):
        key_value = jnp.dot(
            normed,
            kvw[:, head * (NOPE + VDIM) : (head + 1) * (NOPE + VDIM)],
            preferred_element_type=jnp.float32,
        ).astype(bf16)
        keys = jnp.concatenate([key_value[:, :NOPE], key_rope], axis=1)
        values = key_value[:, NOPE:]
        nope = query[:, head * HEAD : head * HEAD + NOPE].astype(bf16)
        rope = turn(query[:, head * HEAD + NOPE : (head + 1) * HEAD], table[rows:, :])
        queries = jnp.concatenate([nope, rope.astype(bf16)], axis=1)
        for block in range(2):
            window = slice(rows * block, rows * (block + 2))
            scores = dot_transposed(queries[rows * block : rows * (block + 1)], keys[window])
            scores = scores * (HEAD ** (-0.5)) + bias[block]
            weights = jnp.exp(scores - jnp.max(scores, axis=-1, keepdims=True))
            total = jnp.sum(weights, axis=-1, keepdims=True)
            mixed = jnp.dot(
                weights.astype(bf16), values[window], preferred_element_type=jnp.float32
            )
            out[block, :, head * VDIM : (head + 1) * VDIM] = (mixed * (1.0 / total)).astype(bf16)


def attend(ql, kvl, qw, kvw, gain, table, query_docs, key_docs):
    tokens = ql.shape[0]
    heads = qw.shape[1] // HEAD
    return pl.pallas_call(
        attend_kernel,
        out_shape=jax.ShapeDtypeStruct((2, tokens // 2, heads * VDIM), jnp.bfloat16),
        in_specs=[VM] * 8,
        out_specs=VM,
        scratch_shapes=[
            pltpu.VMEM((tokens, qw.shape[1]), jnp.float32),
            pltpu.VMEM((2, tokens // 2, tokens), jnp.float32),
        ],
        compiler_params=pltpu.CompilerParams(vmem_limit_bytes=40 << 20),
        name="attend",
    )(ql, kvl, qw, kvw, gain, table, query_docs, key_docs)


def project_kernel(
    att,
    ow,
    out,
    every,
    kept,
    given,
    taken,
    summed,
    inbox,
    reduced,
    moved,
    final,
    send_sems,
    recv_sems,
    part_send,
    part_recv,
    move_send,
    move_recv,
    last,
):
    me = Place()
    peer = me.at(y=1 - me.y)
    twin = me.at(core=1 - me.core)
    fellows = [me.at(chip=(me.chip + step) % Z) for step in range(1, Z)]
    column = [me.at(z=(me.z + step) % Z) for step in range(1, Z)]
    enter([peer, twin] + fellows + column)
    sends = Sends(send_sems, recv_sems)
    depth = att.shape[2]
    rows = out.shape[0] // Z
    mine = pl.ds(pl.multiple_of(me.chip * rows, rows), rows)

    def views(z, part):
        return [every.at[z, me.y if part == 0 else 1 - me.y]]

    ring = Ring(sends, me, views)
    swap = sends.slot()
    sends.start(swap, att.at[1 - me.y], every.at[me.z, me.y], peer)
    own = [att.at[me.y]]
    ring.send(0, 1, 0, own)
    ring.send(1, 1, 0, own)
    twins = [sends.slot() for _ in range(Z)]

    def remote(source, target, send, recv, device):
        return pltpu.make_async_remote_copy(
            source, target, send, recv, device_id=device, device_id_type=MESH
        )

    def product(first, second, which):
        near = pl.ds(pl.multiple_of(me.y * depth, depth), depth)
        far = pl.ds(pl.multiple_of((1 - me.y) * depth, depth), depth)
        return dot_transposed(first, ow[which, :, near]) + dot_transposed(second, ow[which, :, far])

    def tile(number):
        z = (me.z + OFFSETS[number]) % Z
        first = att[me.y] if number == 0 else every[z, me.y]
        second = every[z, 1 - me.y]
        given[number] = product(first, second, 1 - me.core).astype(jnp.bfloat16)
        sends.start(twins[number], given.at[number], taken.at[number], twin)
        kept[number % 2] = product(first, second, me.core)

    def spread(number):
        sends.arrived(twins[number], taken.at[number], twin)
        summed[number] = (kept[number % 2] + taken[number].astype(jnp.float32)).astype(jnp.bfloat16)
        for step in range(1, Z):
            chip = (me.chip + step) % Z
            part = pl.ds(pl.multiple_of(chip * rows, rows), rows)
            remote(
                summed.at[number, part],
                inbox.at[number, step - 1],
                part_send.at[number],
                part_recv.at[number],
                fellows[step - 1],
            ).start()

    def parts(number):
        return remote(
            inbox.at[number], inbox.at[number], part_send.at[number], part_recv.at[number], peer
        )

    def move(number):
        return remote(
            reduced.at[number],
            moved.at[number],
            move_send.at[number],
            move_recv.at[number],
            me.at(z=(me.z + OFFSETS[number]) % Z),
        )

    def finish(number):
        parts(number).wait_recv()
        total = summed[number, mine, :].astype(jnp.float32)
        for source in range(Z - 1):
            total = total + inbox[number, source].astype(jnp.float32)
        if number == 0:
            moved[0] = total.astype(jnp.bfloat16)
        else:
            reduced[number] = total.astype(jnp.bfloat16)
            move(number).start()

    def deliver(number):
        if number:
            move(number).wait_recv()
        chip = (me.z + Z - OFFSETS[number]) % Z

        @pl.when(chip == me.chip)
        def _():
            final[mine, :] = moved[number]

        @pl.when(chip != me.chip)
        def _():
            remote(
                moved.at[number], final.at[mine], last.at[0], last.at[1], me.at(chip=chip)
            ).start()

    sends.arrived(swap, every.at[me.z, 1 - me.y], peer)
    ring.send(0, 1, 1, None)
    ring.send(1, 1, 1, None)
    tile(0)
    for steps in range(1, 4):
        for part in (0, 1):
            ring.arrive(0, steps, part)
            ring.arrive(1, steps, part)
        for number in (2 * steps - 1, 2 * steps):
            spread(number - 1)
            tile(number)
            if number >= 3:
                finish(number - 3)
    spread(6)
    finish(4)
    for number in range(3):
        deliver(number)
    ring.arrive(0, 4, 0)
    ring.arrive(1, 4, 1)
    tile(7)
    finish(5)
    spread(7)
    finish(6)
    deliver(3)
    deliver(4)
    finish(7)
    deliver(5)
    deliver(6)
    deliver(7)
    sends.drain()
    for number in range(Z):
        parts(number).wait_send()
        if number:
            move(number).wait_send()
    everyone = final.at[pl.ds(0, rows * (Z - 1))]
    remote(everyone, everyone, last.at[0], last.at[1], peer).wait()
    out[...] = final[...]


def project(att, ow):
    _, rows, depth = att.shape
    columns = ow.shape[1]
    part = rows // Z
    bf16 = jnp.bfloat16
    return pl.pallas_call(
        project_kernel,
        out_shape=jax.ShapeDtypeStruct((rows, columns), bf16),
        in_specs=[VM] * 2,
        out_specs=VM,
        scratch_shapes=[
            pltpu.VMEM((Z, 2, rows, depth), bf16),
            pltpu.VMEM((2, rows, columns), jnp.float32),
            pltpu.VMEM((Z, rows, columns), bf16),
            pltpu.VMEM((Z, rows, columns), bf16),
            pltpu.VMEM((Z, rows, columns), bf16),
            pltpu.VMEM((Z, Z - 1, part, columns), bf16),
            pltpu.VMEM((Z, part, columns), bf16),
            pltpu.VMEM((Z, part, columns), bf16),
            pltpu.VMEM((rows, columns), bf16),
            pltpu.SemaphoreType.DMA((32,)),
            pltpu.SemaphoreType.DMA((32,)),
            pltpu.SemaphoreType.DMA((Z,)),
            pltpu.SemaphoreType.DMA((Z,)),
            pltpu.SemaphoreType.DMA((Z,)),
            pltpu.SemaphoreType.DMA((Z,)),
            pltpu.SemaphoreType.DMA((2,)),
        ],
        compiler_params=pltpu.CompilerParams(
            collective_id=1, has_side_effects=True, vmem_limit_bytes=40 << 20
        ),
        name="project",
    )(att, ow)


def per_device(q_latent, kv_latent, kv_gain, q_weight, kv_weight, out_weight, documents):
    rows = q_latent.shape[0]
    z = lax.axis_index("ctx") // 2
    ql, kvl, qw, kvw, ow = gather(q_latent, kv_latent.T, q_weight, kv_weight, out_weight.T)
    positions = z * 2 * rows - rows + jnp.arange(3 * rows, dtype=jnp.int32)
    inverse = 10000.0 ** (-2.0 * jnp.arange(ROPE // 2, dtype=jnp.float32) / ROPE)
    angles = positions.astype(jnp.float32)[:, None] * inverse[None, :]
    cosine, sine = jnp.cos(angles), jnp.sin(angles)
    table = jnp.concatenate([cosine, cosine, -sine, sine], axis=1)
    padded = jnp.concatenate([jnp.full((rows,), -1, jnp.int32), documents])
    key_docs = lax.dynamic_slice_in_dim(padded, z * 2 * rows, 3 * rows, 0)
    att = attend(
        ql.reshape(2 * rows, -1),
        kvl,
        qw.reshape(-1, qw.shape[2]),
        kvw.reshape(-1, kvw.shape[2]),
        kv_gain[None, :],
        table,
        key_docs[rows:, None],
        key_docs[None, :],
    )
    return project(att, ow)


def solution(mesh):
    return jax.shard_map(
        per_device,
        mesh=mesh,
        in_specs=(
            P("ctx", None),
            P("ctx", None),
            P(),
            P("ctx", "grp"),
            P("ctx", "grp"),
            P("grp", "ctx"),
            P(),
        ),
        out_specs=P("ctx", "grp"),
        check_vma=False,
    )
```

```python
import jax
import jax.numpy as jnp
from jax import lax
from jax.experimental import pallas as pl
from jax.experimental.pallas import tpu as pltpu
from jax.sharding import PartitionSpec as P

KL = 512
NOPE = 128
ROPE = 64
VDIM = 128
HEAD = NOPE + ROPE
Z = 8
MESH = pl.DeviceIdType.MESH
VM = pl.BlockSpec(memory_space=pltpu.VMEM)
EPSILON = 1e-06
OFFSETS = [0, 7, 1, 6, 2, 5, 3, 4]


class Place:
    def __init__(self):
        ctx = lax.axis_index("ctx")
        grp = lax.axis_index("grp")
        self.ctx = ctx
        self.z = ctx // 2
        self.y = ctx % 2
        self.chip = grp // 2
        self.core = grp % 2

    def at(self, z=None, y=None, chip=None, core=None):
        z = self.z if z is None else z
        y = self.y if y is None else y
        chip = self.chip if chip is None else chip
        core = self.core if core is None else core
        return (z * 2 + y, chip * 2 + core)


class Sends:
    def __init__(self, send_sems, recv_sems):
        self.send_sems = send_sems
        self.recv_sems = recv_sems
        self.used = 0
        self.started = []

    def slot(self):
        self.used += 1
        return self.used - 1

    def make(self, number, source, target, device):
        return pltpu.make_async_remote_copy(
            source,
            target,
            self.send_sems.at[number],
            self.recv_sems.at[number],
            device_id=device,
            device_id_type=MESH,
        )

    def start(self, number, source, target, device):
        copy = self.make(number, source, target, device)
        copy.start()
        self.started.append(copy)

    def arrived(self, number, target, device):
        self.make(number, target, target, device).wait_recv()

    def drain(self):
        for copy in self.started:
            copy.wait_send()


def enter(devices):
    barrier = pltpu.get_barrier_semaphore()
    for device in devices:
        pl.semaphore_signal(barrier, inc=1, device_id=device, device_id_type=MESH)
    pl.semaphore_wait(barrier, len(devices))


class Ring:
    def __init__(self, sends, place, views):
        self.sends = sends
        self.place = place
        self.views = views
        self.up = place.at(z=(place.z + 1) % Z)
        self.down = place.at(z=(place.z + Z - 1) % Z)
        self.slots = {}

    def number(self, way, steps, part, which):
        key = (way, steps, part, which)
        if key not in self.slots:
            self.slots[key] = self.sends.slot()
        return self.slots[key]

    def reach(self, way, part):
        return 4 if (way == 0) == (part == 0) else 3

    def send(self, way, steps, part, sources):
        if steps > self.reach(way, part):
            return
        origin = (self.place.z + (Z - steps + 1 if way == 0 else steps - 1)) % Z
        targets = self.views(origin, part)
        for which, (source, target) in enumerate(zip(sources or targets, targets)):
            self.sends.start(
                self.number(way, steps, part, which),
                source,
                target,
                self.up if way == 0 else self.down,
            )

    def arrive(self, way, steps, part):
        if steps > self.reach(way, part):
            return
        origin = (self.place.z + (Z - steps if way == 0 else steps)) % Z
        for which, target in enumerate(self.views(origin, part)):
            self.sends.arrived(self.number(way, steps, part, which), target, self.up)
        self.send(way, steps + 1, part, None)


def dot(left, right):
    return jnp.dot(left, right, preferred_element_type=jnp.float32)


def dot_transposed(left, right):
    return lax.dot_general(
        left, right, (((1,), (1,)), ((), ())), preferred_element_type=jnp.float32
    )


def turn(inputs, table):
    half = ROPE // 2
    swapped = jnp.concatenate([inputs[:, half:], inputs[:, :half]], axis=1)
    return inputs * table[:, :ROPE] + swapped * table[:, ROPE:]


def layer_kernel(
    ql,
    kvl,
    qw,
    kvw,
    ow,
    gain,
    inverse,
    documents,
    out,
    all_ql,
    all_kvl,
    all_qw,
    all_kvw,
    all_ow,
    docs,
    table,
    bias,
    normed,
    key_rope,
    query,
    key_value,
    att,
    every,
    kept,
    given,
    taken,
    summed,
    inbox,
    reduced,
    moved,
    final,
    send_sems,
    recv_sems,
    local_sems,
    part_send,
    part_recv,
    move_send,
    move_recv,
    last,
):
    bf16 = jnp.bfloat16
    me = Place()
    peer = me.at(y=1 - me.y)
    twin = me.at(core=1 - me.core)
    fellows = [me.at(chip=(me.chip + step) % Z) for step in range(1, Z)]
    column = [me.at(z=(me.z + step) % Z) for step in range(1, Z)]
    above = column[0]
    enter([peer, twin] + fellows + column)
    sends = Sends(send_sems, recv_sems)
    tokens = ql.shape[0]
    deep_q, deep_kv = qw.shape[0], kvw.shape[0]
    wide_q, wide_kv = qw.shape[1] // 4, kvw.shape[1] // 4
    depth = att.shape[3]
    rows = out.shape[0] // Z
    mine = pl.ds(pl.multiple_of(me.chip * rows, rows), rows)

    def remote(source, target, send, recv, device):
        return pltpu.make_async_remote_copy(
            source, target, send, recv, device_id=device, device_id_type=MESH
        )

    def slab(array, pair, row, deep):
        return array.at[pair, pl.ds(pl.multiple_of(row * deep, deep), deep)]

    def weight_views(pair):
        def views(origin, part):
            row = origin * 2 + (me.y if part == 0 else 1 - me.y)
            return [slab(all_qw, pair, row, deep_q), slab(all_kvw, pair, row, deep_kv)]

        return views

    def cut(y, pair):
        number = y * 2 + pair
        return [
            qw.at[:, pl.ds(pl.multiple_of(number * wide_q, 128), wide_q)],
            kvw.at[:, pl.ds(pl.multiple_of(number * wide_kv, 128), wide_kv)],
        ]

    def attended_views(pair):
        def views(origin, part):
            return [every.at[pair, origin, me.y if part == 0 else 1 - me.y]]

        return views

    weights = [Ring(sends, me, weight_views(pair)) for pair in range(2)]
    results = [Ring(sends, me, attended_views(pair)) for pair in range(2)]
    swaps = [[sends.slot(), sends.slot()] for _ in range(2)]
    backs = [sends.slot() for _ in range(2)]
    twins = [sends.slot() for _ in range(Z)]
    lat_q, lat_kv, twin_q, twin_kv, prior, twin_prior, swap_out = (sends.slot() for _ in range(7))

    def both(ring, steps, part):
        ring.arrive(0, steps, part)
        ring.arrive(1, steps, part)

    def begin(ring, part, sources):
        ring.send(0, 1, part, sources)
        ring.send(1, 1, part, sources)

    def swap_weights(pair):
        for number, source, target in zip(
            swaps[pair], cut(1 - me.y, pair), weights[pair].views(me.z, 0)
        ):
            sends.start(number, source, target, peer)

    def swapped_weights(pair):
        for number, target in zip(swaps[pair], weights[pair].views(me.z, 1)):
            sends.arrived(number, target, peer)

    half = tokens // 2
    near = pl.ds(pl.multiple_of(me.core * half, half), half)
    far = pl.ds(pl.multiple_of((1 - me.core) * half, half), half)

    def make_tables():
        docs[:, :tokens] = jnp.full((1, tokens), -1.0, jnp.float32)
        docs[:, tokens:] = documents[...].astype(jnp.float32)
        key_docs = docs[:, pl.ds(pl.multiple_of(me.z * 2 * tokens, 128), 3 * tokens)]
        query_docs = jnp.broadcast_to(key_docs[:, tokens:], (128, 2 * tokens)).T
        for block in range(2):
            shape = (tokens, 2 * tokens)
            spot_q = lax.broadcasted_iota(jnp.int32, shape, 0)
            spot_k = lax.broadcasted_iota(jnp.int32, shape, 1)
            same = (
                query_docs[tokens * block : tokens * (block + 1), :1]
                == key_docs[:, tokens * block : tokens * (block + 2)]
            )
            bias[block] = jnp.where(same & (spot_k - tokens <= spot_q), 0.0, -1e30)
        first = me.z * 2 * tokens - tokens
        spots = (first + lax.broadcasted_iota(jnp.int32, (3 * tokens, 128), 0)).astype(jnp.float32)
        angles = spots * inverse[...]
        lane = lax.broadcasted_iota(jnp.int32, (3 * tokens, 128), 1)
        sine = jnp.sin(angles)
        table[...] = jnp.where(
            lane < ROPE, jnp.cos(angles), jnp.where(lane < ROPE + ROPE // 2, -sine, sine)
        )

    def make_keys():
        latents = jnp.concatenate(
            [all_kvl[number].astype(jnp.float32).T for number in range(3)], axis=0
        )
        latent = latents[:, :KL]
        scale = lax.rsqrt(jnp.mean(latent * latent, axis=-1, keepdims=True) + EPSILON)
        normed[...] = (latent * scale * gain[...]).astype(bf16)
        key_rope[...] = turn(latents[:, KL:], table[...]).astype(bf16)

    def make_pair(pair):
        for block in range(2):
            query[tokens * block : tokens * (block + 1), :] = dot(all_ql[block], all_qw[pair])
        key_value[...] = dot(normed[...], all_kvw[pair]).astype(bf16)

    def attend(pair, head):
        start = head * (NOPE + VDIM)
        keys = jnp.concatenate([key_value[:, start : start + NOPE], key_rope[...]], axis=1)
        values = key_value[:, start + NOPE : start + NOPE + VDIM]
        nope = query[:, head * HEAD : head * HEAD + NOPE].astype(bf16)
        rope = turn(query[:, head * HEAD + NOPE : (head + 1) * HEAD], table[tokens:, :])
        queries = jnp.concatenate([nope, rope.astype(bf16)], axis=1)
        for block in range(2):
            window = slice(tokens * block, tokens * (block + 2))
            scores = dot_transposed(queries[tokens * block : tokens * (block + 1)], keys[window])
            scores = scores * (HEAD ** (-0.5)) + bias[block]
            powers = jnp.exp(scores - jnp.max(scores, axis=-1, keepdims=True))
            total = jnp.sum(powers, axis=-1, keepdims=True)
            mixed = dot(powers.astype(bf16), values[window]) * (1.0 / total)
            att[pair, block, :, head * VDIM : (head + 1) * VDIM] = mixed.astype(bf16)

    def swap_attended(pair):
        sends.start(backs[pair], att.at[pair, 1 - me.y], every.at[pair, me.z, me.y], peer)

    def swapped_attended(pair):
        sends.arrived(backs[pair], every.at[pair, me.z, 1 - me.y], peer)

    def product(number, z, which):
        total = None
        for y in (me.y, 1 - me.y):
            for pair in range(2):
                if number == 0 and y is me.y:
                    left = att[pair, y]
                else:
                    left = every[pair, z, y]
                part = pl.ds(pl.multiple_of((y * 2 + pair) * depth, depth), depth)
                term = dot_transposed(left, all_ow[which, :, part])
                total = term if total is None else total + term
        return total

    def tile(number):
        z = (me.z + OFFSETS[number]) % Z
        given[number] = product(number, z, 1 - me.core).astype(bf16)
        sends.start(twins[number], given.at[number], taken.at[number], twin)
        kept[number % 2] = product(number, z, me.core)

    def spread(number):
        sends.arrived(twins[number], taken.at[number], twin)
        summed[number] = (kept[number % 2] + taken[number].astype(jnp.float32)).astype(bf16)
        for step in range(1, Z):
            chip = (me.chip + step) % Z
            part = pl.ds(pl.multiple_of(chip * rows, rows), rows)
            remote(
                summed.at[number, part],
                inbox.at[number, step - 1],
                part_send.at[number],
                part_recv.at[number],
                fellows[step - 1],
            ).start()

    def parts(number):
        return remote(
            inbox.at[number], inbox.at[number], part_send.at[number], part_recv.at[number], peer
        )

    def move(number):
        return remote(
            reduced.at[number],
            moved.at[number],
            move_send.at[number],
            move_recv.at[number],
            me.at(z=(me.z + OFFSETS[number]) % Z),
        )

    def finish(number):
        parts(number).wait_recv()
        total = summed[number, mine, :].astype(jnp.float32)
        for source in range(Z - 1):
            total = total + inbox[number, source].astype(jnp.float32)
        if number == 0:
            moved[0] = total.astype(bf16)
        else:
            reduced[number] = total.astype(bf16)
            move(number).start()

    def deliver(number):
        if number:
            move(number).wait_recv()
        chip = (me.z + Z - OFFSETS[number]) % Z

        @pl.when(chip == me.chip)
        def _():
            final[mine, :] = moved[number]

        @pl.when(chip != me.chip)
        def _():
            remote(
                moved.at[number], final.at[mine], last.at[0], last.at[1], me.at(chip=chip)
            ).start()

    swap_weights(0)
    begin(weights[0], 0, cut(me.y, 0))
    local = []
    for source, target in [
        (cut(me.y, 0)[0], weights[0].views(me.z, 0)[0]),
        (cut(me.y, 0)[1], weights[0].views(me.z, 0)[1]),
        (cut(me.y, 1)[0], weights[1].views(me.z, 0)[0]),
        (cut(me.y, 1)[1], weights[1].views(me.z, 0)[1]),
        (kvl, all_kvl.at[1 + me.y]),
        (ql, all_ql.at[me.y]),
        (ow, all_ow.at[me.y]),
    ]:
        copy = pltpu.make_async_copy(source, target, local_sems.at[len(local)])
        copy.start()
        local.append(copy)
    sends.start(lat_kv, kvl.at[:, near], all_kvl.at[1 + me.y, :, near], peer)
    sends.start(lat_q, ql.at[near], all_ql.at[me.y, near], peer)
    swapped_weights(0)
    begin(weights[0], 1, None)
    swap_weights(1)
    make_tables()
    both(weights[0], 1, 0)
    sends.start(swap_out, ow, all_ow.at[me.y], peer)
    local[4].wait()
    sends.arrived(lat_kv, all_kvl.at[2 - me.y, :, near], peer)
    sends.start(prior, all_kvl.at[2, :, near], all_kvl.at[0, :, near], above)
    sends.start(
        twin_kv, all_kvl.at[2 - me.y, :, near], all_kvl.at[2 - me.y, :, near], twin
    )
    both(weights[0], 1, 1)
    sends.arrived(lat_q, all_ql.at[1 - me.y, near], peer)
    sends.start(twin_q, all_ql.at[1 - me.y, near], all_ql.at[1 - me.y, near], twin)
    both(weights[0], 2, 0)
    sends.arrived(prior, all_kvl.at[0, :, near], above)
    sends.start(twin_prior, all_kvl.at[0, :, near], all_kvl.at[0, :, near], twin)
    both(weights[0], 2, 1)
    both(weights[0], 3, 0)
    both(weights[0], 3, 1)
    begin(weights[1], 0, cut(me.y, 1))
    swapped_weights(1)
    begin(weights[1], 1, None)
    sends.arrived(twin_kv, all_kvl.at[2 - me.y, :, far], twin)
    sends.arrived(twin_prior, all_kvl.at[0, :, far], twin)
    make_keys()
    both(weights[0], 4, 0)
    both(weights[0], 4, 1)
    sends.arrived(twin_q, all_ql.at[1 - me.y, far], twin)
    for number in (0, 1, 5):
        local[number].wait()
    make_pair(0)
    both(weights[1], 1, 0)
    both(weights[1], 1, 1)
    attend(0, 0)
    both(weights[1], 2, 0)
    attend(0, 1)
    swap_attended(0)
    begin(results[0], 0, [att.at[0, me.y]])
    both(weights[1], 2, 1)
    both(weights[1], 3, 0)
    both(weights[1], 3, 1)
    swapped_attended(0)
    begin(results[0], 1, None)
    both(weights[1], 4, 0)
    both(weights[1], 4, 1)
    for number in (2, 3):
        local[number].wait()
    make_pair(1)
    both(results[0], 1, 0)
    attend(1, 0)
    both(results[0], 1, 1)
    attend(1, 1)
    swap_attended(1)
    begin(results[1], 0, [att.at[1, me.y]])
    both(results[0], 2, 0)
    both(results[0], 2, 1)
    swapped_attended(1)
    begin(results[1], 1, None)
    local[6].wait()
    sends.arrived(swap_out, all_ow.at[1 - me.y], peer)
    tile(0)
    for steps in range(1, 4):
        for part in (0, 1):
            if steps == 1:
                both(results[0], 3, part)
            both(results[1], steps, part)
            if steps == 2:
                both(results[0], 4, part)
        for number in (2 * steps - 1, 2 * steps):
            spread(number - 1)
            tile(number)
            if number >= 3:
                finish(number - 3)
    spread(6)
    finish(4)
    for number in range(3):
        deliver(number)
    both(results[1], 4, 0)
    both(results[1], 4, 1)
    tile(7)
    finish(5)
    spread(7)
    finish(6)
    deliver(3)
    deliver(4)
    finish(7)
    deliver(5)
    deliver(6)
    deliver(7)
    sends.drain()
    for number in range(Z):
        parts(number).wait_send()
        if number:
            move(number).wait_send()
    everyone = final.at[pl.ds(0, rows * (Z - 1))]
    remote(everyone, everyone, last.at[0], last.at[1], peer).wait()
    out[...] = final[...]


def per_device(q_latent, kv_latent, kv_gain, q_weight, kv_weight, out_weight, documents):
    tokens = q_latent.shape[0]
    columns = out_weight.shape[1]
    ctx = lax.axis_size("ctx")
    wide_q, wide_kv = q_weight.shape[1] // 4, kv_weight.shape[1] // 4
    depth = 2 * VDIM
    part = tokens // Z
    bf16, f32 = jnp.bfloat16, jnp.float32
    spot = jnp.arange(128, dtype=f32) % (ROPE // 2)
    inverse = (10000.0 ** (-2.0 * spot / ROPE))[None, :]
    return pl.pallas_call(
        layer_kernel,
        out_shape=jax.ShapeDtypeStruct((tokens, columns), bf16),
        in_specs=[VM] * 8,
        out_specs=VM,
        scratch_shapes=[
            pltpu.VMEM((2, tokens, q_latent.shape[1]), bf16),
            pltpu.VMEM((3, kv_latent.shape[1], tokens), bf16),
            pltpu.VMEM((2, ctx * q_weight.shape[0], wide_q), bf16),
            pltpu.VMEM((2, ctx * kv_weight.shape[0], wide_kv), bf16),
            pltpu.VMEM((2, columns, out_weight.shape[0]), bf16),
            pltpu.VMEM((1, documents.shape[0] + tokens), f32),
            pltpu.VMEM((3 * tokens, 128), f32),
            pltpu.VMEM((2, tokens, 2 * tokens), f32),
            pltpu.VMEM((3 * tokens, KL), bf16),
            pltpu.VMEM((3 * tokens, ROPE), bf16),
            pltpu.VMEM((2 * tokens, wide_q), f32),
            pltpu.VMEM((3 * tokens, wide_kv), bf16),
            pltpu.VMEM((2, 2, tokens, depth), bf16),
            pltpu.VMEM((2, Z, 2, tokens, depth), bf16),
            pltpu.VMEM((2, tokens, columns), f32),
            pltpu.VMEM((Z, tokens, columns), bf16),
            pltpu.VMEM((Z, tokens, columns), bf16),
            pltpu.VMEM((Z, tokens, columns), bf16),
            pltpu.VMEM((Z, Z - 1, part, columns), bf16),
            pltpu.VMEM((Z, part, columns), bf16),
            pltpu.VMEM((Z, part, columns), bf16),
            pltpu.VMEM((tokens, columns), bf16),
            pltpu.SemaphoreType.DMA((112,)),
            pltpu.SemaphoreType.DMA((112,)),
            pltpu.SemaphoreType.DMA((7,)),
            pltpu.SemaphoreType.DMA((Z,)),
            pltpu.SemaphoreType.DMA((Z,)),
            pltpu.SemaphoreType.DMA((Z,)),
            pltpu.SemaphoreType.DMA((Z,)),
            pltpu.SemaphoreType.DMA((2,)),
        ],
        compiler_params=pltpu.CompilerParams(
            collective_id=0, has_side_effects=True, vmem_limit_bytes=50 << 20
        ),
        name="layer",
    )(
        q_latent,
        kv_latent.T,
        q_weight,
        kv_weight,
        out_weight.T,
        kv_gain[None, :],
        inverse,
        documents[None, :],
    )


def solution(mesh):
    return jax.shard_map(
        per_device,
        mesh=mesh,
        in_specs=(
            P("ctx", None),
            P("ctx", None),
            P(),
            P("ctx", "grp"),
            P("ctx", "grp"),
            P("grp", "ctx"),
            P(),
        ),
        out_specs=P("ctx", "grp"),
        check_vma=False,
    )
```

```python
import jax
import jax.numpy as jnp
from jax import lax
from jax.experimental import pallas as pl
from jax.experimental.pallas import tpu as pltpu
from jax.sharding import PartitionSpec as P

KL = 512
NOPE = 128
ROPE = 64
VDIM = 128
HEAD = NOPE + ROPE
Z = 8
MESH = pl.DeviceIdType.MESH
VM = pl.BlockSpec(memory_space=pltpu.VMEM)
HBM = pl.BlockSpec(memory_space=pltpu.HBM)
EPSILON = 1e-06
OFFSETS = [0, 7, 1, 6, 2, 5, 3, 4]


class Place:
    def __init__(self):
        ctx = lax.axis_index("ctx")
        grp = lax.axis_index("grp")
        self.ctx = ctx
        self.z = ctx // 2
        self.y = ctx % 2
        self.chip = grp // 2
        self.core = grp % 2

    def at(self, z=None, y=None, chip=None, core=None):
        z = self.z if z is None else z
        y = self.y if y is None else y
        chip = self.chip if chip is None else chip
        core = self.core if core is None else core
        return (z * 2 + y, chip * 2 + core)


class Sends:
    def __init__(self, send_sems, recv_sems):
        self.send_sems = send_sems
        self.recv_sems = recv_sems
        self.used = 0
        self.groups = 0

    def slot(self):
        self.used += 1
        return self.used - 1

    def group(self):
        self.groups += 1
        return self.groups - 1

    def make(self, group, number, source, target, device):
        return pltpu.make_async_remote_copy(
            source,
            target,
            self.send_sems.at[group],
            self.recv_sems.at[number],
            device_id=device,
            device_id_type=MESH,
        )

    def start(self, group, number, source, target, device):
        self.make(group, number, source, target, device).start()

    def arrived(self, number, target, device):
        self.make(0, number, target, target, device).wait_recv()

    def sent(self, group, volume, device):
        self.make(group, 0, volume, volume, device).wait_send()


def enter(devices):
    barrier = pltpu.get_barrier_semaphore()
    for device in devices:
        pl.semaphore_signal(barrier, inc=1, device_id=device, device_id_type=MESH)
    pl.semaphore_wait(barrier, len(devices))


class Ring:
    def __init__(self, sends, place, views, groups):
        self.sends = sends
        self.groups = groups
        self.place = place
        self.views = views
        self.up = place.at(z=(place.z + 1) % Z)
        self.down = place.at(z=(place.z + Z - 1) % Z)
        self.slots = {}

    def number(self, way, steps, part, which):
        key = (way, steps, part, which)
        if key not in self.slots:
            self.slots[key] = self.sends.slot()
        return self.slots[key]

    def reach(self, way, part):
        return 4 if (way == 0) == (part == 0) else 3

    def send(self, way, steps, part, sources):
        if steps > self.reach(way, part):
            return
        origin = (self.place.z + (Z - steps + 1 if way == 0 else steps - 1)) % Z
        targets = self.views(origin, part)
        for which, (source, target) in enumerate(zip(sources or targets, targets)):
            self.sends.start(
                self.groups[which],
                self.number(way, steps, part, which),
                source,
                target,
                self.up if way == 0 else self.down,
            )

    def arrive(self, way, steps, part):
        if steps > self.reach(way, part):
            return
        origin = (self.place.z + (Z - steps if way == 0 else steps)) % Z
        for which, target in enumerate(self.views(origin, part)):
            self.sends.arrived(self.number(way, steps, part, which), target, self.up)
        self.send(way, steps + 1, part, None)


def dot(left, right):
    return jnp.dot(left, right, preferred_element_type=jnp.float32)


def dot_transposed(left, right):
    return lax.dot_general(
        left, right, (((1,), (1,)), ((), ())), preferred_element_type=jnp.float32
    )


def turn(inputs, table):
    half = ROPE // 2
    swapped = jnp.concatenate([inputs[:, half:], inputs[:, :half]], axis=1)
    return inputs * table[:, :ROPE] + swapped * table[:, ROPE:]


def layer_kernel(
    ql_in,
    kvl_in,
    qw_in,
    kvw_in,
    ow_in,
    gain_in,
    documents_in,
    inverse,
    out,
    qw,
    kvw,
    gain,
    documents,
    all_ql,
    all_kvl,
    all_qw,
    all_kvw,
    all_ow,
    docs,
    table,
    bias,
    normed,
    key_rope,
    query,
    key_value,
    att,
    every,
    kept,
    given,
    taken,
    summed,
    inbox,
    reduced,
    moved,
    final,
    send_sems,
    recv_sems,
    local_sems,
    own_sems,
    part_send,
    part_recv,
    move_send,
    move_recv,
    last,
):
    bf16 = jnp.bfloat16
    me = Place()
    peer = me.at(y=1 - me.y)
    twin = me.at(core=1 - me.core)
    fellows = [me.at(chip=(me.chip + step) % Z) for step in range(1, Z)]
    column = [me.at(z=(me.z + step) % Z) for step in range(1, Z)]
    above = column[0]
    local = []
    for number, (source, target) in enumerate(
        [
            (qw_in, qw),
            (kvw_in, kvw),
            (kvl_in, all_kvl.at[1 + me.y]),
            (ql_in, all_ql.at[me.y]),
            (documents_in, documents),
            (gain_in, gain),
            (ow_in, all_ow.at[me.y]),
        ]
    ):
        copy = pltpu.make_async_copy(source, target, local_sems.at[number])
        copy.start()
        local.append(copy)
    enter([peer, twin] + fellows + column)
    for number in (0, 1):
        local[number].wait()
    sends = Sends(send_sems, recv_sems)
    tokens = ql_in.shape[0]
    deep_q, deep_kv = qw.shape[0], kvw.shape[0]
    wide_q, wide_kv = qw.shape[1] // 4, kvw.shape[1] // 4
    depth = att.shape[3]
    rows = out.shape[0] // Z
    mine = pl.ds(pl.multiple_of(me.chip * rows, rows), rows)

    def remote(source, target, send, recv, device):
        return pltpu.make_async_remote_copy(
            source, target, send, recv, device_id=device, device_id_type=MESH
        )

    def slab(array, pair, row, deep):
        return array.at[pair, pl.ds(pl.multiple_of(row * deep, deep), deep)]

    def weight_views(pair):
        def views(origin, part):
            row = origin * 2 + (me.y if part == 0 else 1 - me.y)
            return [slab(all_qw, pair, row, deep_q), slab(all_kvw, pair, row, deep_kv)]

        return views

    def cut(y, pair):
        number = y * 2 + pair
        return [
            qw.at[:, pl.ds(pl.multiple_of(number * wide_q, 128), wide_q)],
            kvw.at[:, pl.ds(pl.multiple_of(number * wide_kv, 128), wide_kv)],
        ]

    def attended_views(pair):
        def views(origin, part):
            return [every.at[pair, origin, me.y if part == 0 else 1 - me.y]]

        return views

    weights = [
        Ring(sends, me, weight_views(pair), [sends.group(), sends.group()]) for pair in range(2)
    ]
    results = [Ring(sends, me, attended_views(pair), [sends.group()]) for pair in range(2)]
    back_groups = [sends.group() for _ in range(2)]
    twin_group, prior_group, lat_q_group, lat_kv_group = (sends.group() for _ in range(4))
    twin_q_group, twin_kv_group, twin_prior_group, out_group = (sends.group() for _ in range(4))
    swaps = [[sends.slot(), sends.slot()] for _ in range(2)]
    backs = [sends.slot() for _ in range(2)]
    twins = [sends.slot() for _ in range(Z)]
    lat_q, lat_kv, twin_q, twin_kv, prior, twin_prior, swap_out = (sends.slot() for _ in range(7))

    def both(ring, steps, part):
        ring.arrive(0, steps, part)
        ring.arrive(1, steps, part)

    def begin(ring, part, sources):
        ring.send(0, 1, part, sources)
        ring.send(1, 1, part, sources)

    def start_weights(pair, part):
        ring = weights[pair]
        if part == 0:
            begin(ring, 0, cut(me.y, pair))
            for number, (source, target) in enumerate(
                zip(cut(me.y, pair), ring.views(me.z, 0))
            ):
                copy = pltpu.make_async_copy(source, target, own_sems.at[2 * pair + number])
                copy.start()
                own.append(copy)
        else:
            for number, target in zip(swaps[pair], ring.views(me.z, 1)):
                sends.arrived(number, target, peer)
            begin(ring, 1, None)

    def swap_weights(pair):
        for group, number, source, target in zip(
            weights[pair].groups, swaps[pair], cut(1 - me.y, pair), weights[pair].views(me.z, 0)
        ):
            sends.start(group, number, source, target, peer)

    def start_results(pair, part):
        ring = results[pair]
        if part == 0:
            sends.start(
                back_groups[pair],
                backs[pair],
                att.at[pair, 1 - me.y],
                every.at[pair, me.z, me.y],
                peer,
            )
            begin(ring, 0, [att.at[pair, me.y]])
        else:
            sends.arrived(backs[pair], every.at[pair, me.z, 1 - me.y], peer)
            begin(ring, 1, None)

    own = []
    half = tokens // 2
    near = pl.ds(pl.multiple_of(me.core * half, half), half)
    far = pl.ds(pl.multiple_of((1 - me.core) * half, half), half)

    def make_tables():
        local[4].wait()
        local[5].wait()
        docs[:, :tokens] = jnp.full((1, tokens), -1.0, jnp.float32)
        docs[:, tokens:] = documents[...].astype(jnp.float32)
        key_docs = docs[:, pl.ds(pl.multiple_of(me.z * 2 * tokens, 128), 3 * tokens)]
        query_docs = jnp.broadcast_to(key_docs[:, tokens:], (128, 2 * tokens)).T
        for block in range(2):
            shape = (tokens, 2 * tokens)
            spot_q = lax.broadcasted_iota(jnp.int32, shape, 0)
            spot_k = lax.broadcasted_iota(jnp.int32, shape, 1)
            same = (
                query_docs[tokens * block : tokens * (block + 1), :1]
                == key_docs[:, tokens * block : tokens * (block + 2)]
            )
            bias[block] = jnp.where(same & (spot_k - tokens <= spot_q), 0.0, -1e30)
        first = me.z * 2 * tokens - tokens
        spots = (first + lax.broadcasted_iota(jnp.int32, (3 * tokens, 128), 0)).astype(jnp.float32)
        angles = spots * inverse[...]
        lane = lax.broadcasted_iota(jnp.int32, (3 * tokens, 128), 1)
        sine = jnp.sin(angles)
        table[...] = jnp.where(
            lane < ROPE, jnp.cos(angles), jnp.where(lane < ROPE + ROPE // 2, -sine, sine)
        )

    def send_latent_kv():
        local[2].wait()
        block = all_kvl.at[1 + me.y, :, near]
        sends.start(lat_kv_group, lat_kv, block, block, peer)

    def send_latent_q():
        local[3].wait()
        block = all_ql.at[me.y, near]
        sends.start(lat_q_group, lat_q, block, block, peer)

    def send_out():
        local[6].wait()
        block = all_ow.at[me.y]
        sends.start(out_group, swap_out, block, block, peer)

    def send_prior():
        block = all_kvl.at[2 - me.y, :, near]
        sends.arrived(lat_kv, block, peer)
        sends.start(
            prior_group, prior, all_kvl.at[2, :, near], all_kvl.at[0, :, near], above
        )
        sends.start(twin_kv_group, twin_kv, block, block, twin)

    def pass_latent_q():
        block = all_ql.at[1 - me.y, near]
        sends.arrived(lat_q, block, peer)
        sends.start(twin_q_group, twin_q, block, block, twin)

    def pass_prior():
        block = all_kvl.at[0, :, near]
        sends.arrived(prior, block, above)
        sends.start(twin_prior_group, twin_prior, block, block, twin)

    def make_keys():
        sends.arrived(twin_kv, all_kvl.at[2 - me.y, :, far], twin)
        sends.arrived(twin_prior, all_kvl.at[0, :, far], twin)
        latents = jnp.concatenate(
            [all_kvl[number].astype(jnp.float32).T for number in range(3)], axis=0
        )
        latent = latents[:, :KL]
        scale = lax.rsqrt(jnp.mean(latent * latent, axis=-1, keepdims=True) + EPSILON)
        normed[...] = (latent * scale * gain[...]).astype(bf16)
        key_rope[...] = turn(latents[:, KL:], table[...]).astype(bf16)

    def make_pair(pair):
        if pair == 0:
            sends.arrived(twin_q, all_ql.at[1 - me.y, far], twin)
        for copy in own[2 * pair : 2 * pair + 2]:
            copy.wait()
        for block in range(2):
            query[tokens * block : tokens * (block + 1), :] = dot(all_ql[block], all_qw[pair])
        key_value[...] = dot(normed[...], all_kvw[pair]).astype(bf16)

    def attend(pair, head):
        start = head * (NOPE + VDIM)
        keys = jnp.concatenate([key_value[:, start : start + NOPE], key_rope[...]], axis=1)
        values = key_value[:, start + NOPE : start + NOPE + VDIM]
        nope = query[:, head * HEAD : head * HEAD + NOPE].astype(bf16)
        rope = turn(query[:, head * HEAD + NOPE : (head + 1) * HEAD], table[tokens:, :])
        queries = jnp.concatenate([nope, rope.astype(bf16)], axis=1)
        for block in range(2):
            window = slice(tokens * block, tokens * (block + 2))
            scores = dot_transposed(queries[tokens * block : tokens * (block + 1)], keys[window])
            scores = scores * (HEAD ** (-0.5)) + bias[block]
            powers = jnp.exp(scores - jnp.max(scores, axis=-1, keepdims=True))
            total = jnp.sum(powers, axis=-1, keepdims=True)
            mixed = dot(powers.astype(bf16), values[window]) * (1.0 / total)
            att[pair, block, :, head * VDIM : (head + 1) * VDIM] = mixed.astype(bf16)

    def product(number, z, which):
        total = None
        for y in (me.y, 1 - me.y):
            for pair in range(2):
                if number == 0 and y is me.y:
                    left = att[pair, y]
                else:
                    left = every[pair, z, y]
                part = pl.ds(pl.multiple_of((y * 2 + pair) * depth, depth), depth)
                term = dot_transposed(left, all_ow[which, :, part])
                total = term if total is None else total + term
        return total

    def tile(number):
        z = (me.z + OFFSETS[number]) % Z
        if number == 0:
            sends.arrived(swap_out, all_ow.at[1 - me.y], peer)
        given[number] = product(number, z, 1 - me.core).astype(bf16)
        sends.start(twin_group, twins[number], given.at[number], taken.at[number], twin)
        kept[number] = product(number, z, me.core)

    def spread(number):
        sends.arrived(twins[number], taken.at[number], twin)
        summed[number] = (kept[number] + taken[number].astype(jnp.float32)).astype(bf16)
        for step in range(1, Z):
            chip = (me.chip + step) % Z
            part = pl.ds(pl.multiple_of(chip * rows, rows), rows)
            remote(
                summed.at[number, part],
                inbox.at[number, step - 1],
                part_send.at[0],
                part_recv.at[number],
                fellows[step - 1],
            ).start()

    def parts(number):
        return remote(
            inbox.at[number], inbox.at[number], part_send.at[0], part_recv.at[number], peer
        )

    def move(number):
        return remote(
            reduced.at[number],
            moved.at[number],
            move_send.at[0],
            move_recv.at[number],
            me.at(z=(me.z + OFFSETS[number]) % Z),
        )

    def finish(number):
        parts(number).wait_recv()
        total = summed[number, mine, :].astype(jnp.float32)
        for source in range(Z - 1):
            total = total + inbox[number, source].astype(jnp.float32)
        if number == 0:
            moved[0] = total.astype(bf16)
        else:
            reduced[number] = total.astype(bf16)
            move(number).start()

    def deliver(number):
        if number:
            move(number).wait_recv()
        chip = (me.z + Z - OFFSETS[number]) % Z

        @pl.when(chip == me.chip)
        def _():
            final[mine, :] = moved[number]

        @pl.when(chip != me.chip)
        def _():
            remote(
                moved.at[number], final.at[mine], last.at[0], last.at[1], me.at(chip=chip)
            ).start()

    swap_weights(0)
    start_weights(0, 0)
    send_latent_kv()
    swap_weights(1)
    send_latent_q()
    start_weights(1, 0)
    start_weights(0, 1)
    weights[0].arrive(1, 1, 0)
    weights[0].arrive(0, 1, 0)
    send_prior()
    weights[0].arrive(1, 1, 1)
    send_out()
    weights[0].arrive(0, 2, 0)
    start_weights(1, 1)
    weights[0].arrive(1, 2, 0)
    make_tables()
    weights[0].arrive(0, 1, 1)
    weights[0].arrive(1, 2, 1)
    weights[1].arrive(1, 1, 0)
    pass_latent_q()
    weights[1].arrive(0, 1, 0)
    weights[0].arrive(0, 3, 0)
    weights[1].arrive(1, 1, 1)
    weights[0].arrive(0, 2, 1)
    weights[1].arrive(0, 2, 0)
    weights[0].arrive(1, 3, 1)
    pass_prior()
    weights[1].arrive(0, 1, 1)
    weights[0].arrive(0, 4, 0)
    weights[1].arrive(1, 2, 1)
    make_keys()
    weights[0].arrive(1, 3, 0)
    weights[1].arrive(1, 2, 0)
    weights[0].arrive(0, 3, 1)
    weights[0].arrive(1, 4, 1)
    make_pair(0)
    weights[1].arrive(0, 3, 0)
    attend(0, 0)
    weights[1].arrive(1, 3, 1)
    attend(0, 1)
    weights[1].arrive(0, 2, 1)
    start_results(0, 0)
    weights[1].arrive(0, 4, 0)
    weights[1].arrive(1, 4, 1)
    weights[1].arrive(1, 3, 0)
    weights[1].arrive(0, 3, 1)
    make_pair(1)
    start_results(0, 1)
    attend(1, 0)
    attend(1, 1)
    start_results(1, 0)
    results[0].arrive(0, 1, 0)
    start_results(1, 1)
    results[1].arrive(1, 1, 0)
    results[1].arrive(0, 1, 0)
    tile(0)
    results[0].arrive(1, 1, 0)
    results[0].arrive(0, 1, 1)
    results[1].arrive(1, 1, 1)
    results[0].arrive(1, 1, 1)
    spread(0)
    results[1].arrive(0, 1, 1)
    tile(2)
    spread(2)
    results[0].arrive(1, 2, 0)
    results[0].arrive(0, 2, 0)
    tile(1)
    results[1].arrive(1, 2, 1)
    results[0].arrive(0, 2, 1)
    results[1].arrive(0, 2, 0)
    spread(1)
    results[1].arrive(0, 2, 1)
    results[0].arrive(1, 2, 1)
    results[1].arrive(1, 2, 0)
    tile(4)
    spread(4)
    tile(3)
    results[1].arrive(0, 3, 0)
    spread(3)
    results[0].arrive(0, 3, 1)
    results[0].arrive(0, 3, 0)
    results[1].arrive(1, 3, 1)
    results[0].arrive(1, 3, 0)
    results[0].arrive(1, 3, 1)
    results[1].arrive(0, 3, 1)
    tile(5)
    finish(4)
    spread(5)
    results[1].arrive(1, 3, 0)
    tile(6)
    finish(1)
    results[1].arrive(0, 4, 0)
    spread(6)
    finish(2)
    results[0].arrive(0, 4, 0)
    results[1].arrive(1, 4, 1)
    results[0].arrive(1, 4, 1)
    tile(7)
    finish(0)
    spread(7)
    finish(6)
    deliver(0)
    finish(3)
    finish(5)
    deliver(1)
    deliver(4)
    deliver(2)
    finish(7)
    deliver(3)
    deliver(6)
    deliver(5)
    deliver(7)
    for pair in range(2):
        group_q, group_kv = weights[pair].groups
        sends.sent(group_q, all_qw.at[pair, pl.ds(0, 15 * deep_q)], peer)
        sends.sent(group_kv, all_kvw.at[pair, pl.ds(0, 15 * deep_kv)], peer)
        sends.sent(results[pair].groups[0], every.at[pair, pl.ds(0, 7)], peer)
        sends.sent(back_groups[pair], att.at[pair, 0], peer)
    sends.sent(twin_group, given, peer)
    for group, volume in [
        (prior_group, all_kvl.at[0, :, near]),
        (lat_q_group, all_ql.at[0, near]),
        (lat_kv_group, all_kvl.at[0, :, near]),
        (twin_q_group, all_ql.at[0, near]),
        (twin_kv_group, all_kvl.at[0, :, near]),
        (twin_prior_group, all_kvl.at[0, :, near]),
        (out_group, all_ow.at[0]),
    ]:
        sends.sent(group, volume, peer)
    remote(inbox, inbox, part_send.at[0], part_recv.at[0], peer).wait_send()
    moves = moved.at[pl.ds(0, Z - 1)]
    remote(moves, moves, move_send.at[0], move_recv.at[0], peer).wait_send()
    everyone = final.at[pl.ds(0, rows * (Z - 1))]
    remote(everyone, everyone, last.at[0], last.at[1], peer).wait()
    out[...] = final[...]


def per_device(q_latent, kv_latent, kv_gain, q_weight, kv_weight, out_weight, documents):
    tokens = q_latent.shape[0]
    columns = out_weight.shape[1]
    ctx = lax.axis_size("ctx")
    wide_q, wide_kv = q_weight.shape[1] // 4, kv_weight.shape[1] // 4
    depth = 2 * VDIM
    part = tokens // Z
    bf16, f32 = jnp.bfloat16, jnp.float32
    spot = jnp.arange(128, dtype=f32) % (ROPE // 2)
    inverse = (10000.0 ** (-2.0 * spot / ROPE))[None, :]
    return pl.pallas_call(
        layer_kernel,
        out_shape=jax.ShapeDtypeStruct((tokens, columns), bf16),
        in_specs=[HBM] * 7 + [VM],
        out_specs=VM,
        scratch_shapes=[
            pltpu.VMEM(q_weight.shape, bf16),
            pltpu.VMEM(kv_weight.shape, bf16),
            pltpu.VMEM((1, kv_gain.shape[0]), f32),
            pltpu.VMEM((1, documents.shape[0]), jnp.int32),
            pltpu.VMEM((2, tokens, q_latent.shape[1]), bf16),
            pltpu.VMEM((3, kv_latent.shape[1], tokens), bf16),
            pltpu.VMEM((2, ctx * q_weight.shape[0], wide_q), bf16),
            pltpu.VMEM((2, ctx * kv_weight.shape[0], wide_kv), bf16),
            pltpu.VMEM((2, columns, out_weight.shape[0]), bf16),
            pltpu.VMEM((1, documents.shape[0] + tokens), f32),
            pltpu.VMEM((3 * tokens, 128), f32),
            pltpu.VMEM((2, tokens, 2 * tokens), f32),
            pltpu.VMEM((3 * tokens, KL), bf16),
            pltpu.VMEM((3 * tokens, ROPE), bf16),
            pltpu.VMEM((2 * tokens, wide_q), f32),
            pltpu.VMEM((3 * tokens, wide_kv), bf16),
            pltpu.VMEM((2, 2, tokens, depth), bf16),
            pltpu.VMEM((2, Z, 2, tokens, depth), bf16),
            pltpu.VMEM((Z, tokens, columns), f32),
            pltpu.VMEM((Z, tokens, columns), bf16),
            pltpu.VMEM((Z, tokens, columns), bf16),
            pltpu.VMEM((Z, tokens, columns), bf16),
            pltpu.VMEM((Z, Z - 1, part, columns), bf16),
            pltpu.VMEM((Z, part, columns), bf16),
            pltpu.VMEM((Z, part, columns), bf16),
            pltpu.VMEM((tokens, columns), bf16),
            pltpu.SemaphoreType.DMA((16,)),
            pltpu.SemaphoreType.DMA((105,)),
            pltpu.SemaphoreType.DMA((7,)),
            pltpu.SemaphoreType.DMA((4,)),
            pltpu.SemaphoreType.DMA((1,)),
            pltpu.SemaphoreType.DMA((Z,)),
            pltpu.SemaphoreType.DMA((1,)),
            pltpu.SemaphoreType.DMA((Z,)),
            pltpu.SemaphoreType.DMA((2,)),
        ],
        compiler_params=pltpu.CompilerParams(
            collective_id=0, has_side_effects=True, vmem_limit_bytes=127 << 19
        ),
        name="layer",
    )(
        q_latent,
        kv_latent.T,
        q_weight,
        kv_weight,
        out_weight.T,
        kv_gain[None, :],
        documents[None, :],
        inverse,
    )


def solution(mesh):
    return jax.shard_map(
        per_device,
        mesh=mesh,
        in_specs=(
            P("ctx", None),
            P("ctx", None),
            P(),
            P("ctx", "grp"),
            P("ctx", "grp"),
            P("grp", "ctx"),
            P(),
        ),
        out_specs=P("ctx", "grp"),
        check_vma=False,
    )
```

```python
import jax
import jax.numpy as jnp
from jax import lax
from jax.experimental import pallas as pl
from jax.experimental.pallas import tpu as pltpu
from jax.sharding import PartitionSpec as P

KL = 512
NOPE = 128
ROPE = 64
VDIM = 128
HEAD = NOPE + ROPE
Z = 8
MESH = pl.DeviceIdType.MESH
VM = pl.BlockSpec(memory_space=pltpu.VMEM)
HBM = pl.BlockSpec(memory_space=pltpu.HBM)
EPSILON = 1e-06
OFFSETS = [0, 7, 1, 6, 2, 5, 3, 4]


class Place:
    def __init__(self):
        ctx = lax.axis_index("ctx")
        grp = lax.axis_index("grp")
        self.ctx = ctx
        self.z = ctx // 2
        self.y = ctx % 2
        self.chip = grp // 2
        self.core = grp % 2

    def at(self, z=None, y=None, chip=None, core=None):
        z = self.z if z is None else z
        y = self.y if y is None else y
        chip = self.chip if chip is None else chip
        core = self.core if core is None else core
        return (z * 2 + y, chip * 2 + core)


class Sends:
    def __init__(self, send_sems, recv_sems):
        self.send_sems = send_sems
        self.recv_sems = recv_sems
        self.used = 0
        self.groups = 0

    def slot(self):
        self.used += 1
        return self.used - 1

    def group(self):
        self.groups += 1
        return self.groups - 1

    def make(self, group, number, source, target, device):
        return pltpu.make_async_remote_copy(
            source,
            target,
            self.send_sems.at[group],
            self.recv_sems.at[number],
            device_id=device,
            device_id_type=MESH,
        )

    def start(self, group, number, source, target, device):
        self.make(group, number, source, target, device).start()

    def arrived(self, number, target, device):
        self.make(0, number, target, target, device).wait_recv()

    def sent(self, group, volume, device):
        self.make(group, 0, volume, volume, device).wait_send()


def enter(devices):
    barrier = pltpu.get_barrier_semaphore()
    for device in devices:
        pl.semaphore_signal(barrier, inc=1, device_id=device, device_id_type=MESH)
    pl.semaphore_wait(barrier, len(devices))


class Ring:
    def __init__(self, sends, place, views, groups):
        self.sends = sends
        self.groups = groups
        self.place = place
        self.views = views
        self.up = place.at(z=(place.z + 1) % Z)
        self.down = place.at(z=(place.z + Z - 1) % Z)
        self.slots = {}

    def number(self, way, steps, part, which):
        key = (way, steps, part, which)
        if key not in self.slots:
            self.slots[key] = self.sends.slot()
        return self.slots[key]

    def reach(self, way, part):
        return 4 if (way == 0) == (part == 0) else 3

    def send(self, way, steps, part, sources):
        if steps > self.reach(way, part):
            return
        origin = (self.place.z + (Z - steps + 1 if way == 0 else steps - 1)) % Z
        targets = self.views(origin, part)
        for which, (source, target) in enumerate(zip(sources or targets, targets)):
            self.sends.start(
                self.groups[which],
                self.number(way, steps, part, which),
                source,
                target,
                self.up if way == 0 else self.down,
            )

    def arrive(self, way, steps, part):
        if steps > self.reach(way, part):
            return
        origin = (self.place.z + (Z - steps if way == 0 else steps)) % Z
        for which, target in enumerate(self.views(origin, part)):
            self.sends.arrived(self.number(way, steps, part, which), target, self.up)
        self.send(way, steps + 1, part, None)


def dot(left, right):
    return jnp.dot(left, right, preferred_element_type=jnp.float32)


def dot_transposed(left, right):
    return lax.dot_general(
        left, right, (((1,), (1,)), ((), ())), preferred_element_type=jnp.float32
    )


def turn(inputs, table):
    half = ROPE // 2
    swapped = jnp.concatenate([inputs[:, half:], inputs[:, :half]], axis=1)
    return inputs * table[:, :ROPE] + swapped * table[:, ROPE:]


def layer_kernel(
    ql_in,
    kvl_in,
    qw_in,
    kvw_in,
    ow_in,
    gain_in,
    documents_in,
    inverse,
    out,
    qw,
    kvw,
    gain,
    documents,
    all_ql,
    all_kvl,
    all_qw,
    all_kvw,
    all_ow,
    docs,
    table,
    bias,
    normed,
    key_rope,
    query,
    key_value,
    att,
    every,
    kept,
    given,
    taken,
    summed,
    inbox,
    reduced,
    moved,
    final,
    ahead,
    send_sems,
    recv_sems,
    local_sems,
    own_sems,
    part_send,
    part_recv,
    move_send,
    move_recv,
    last,
):
    bf16 = jnp.bfloat16
    me = Place()
    peer = me.at(y=1 - me.y)
    twin = me.at(core=1 - me.core)
    fellows = [me.at(chip=(me.chip + step) % Z) for step in range(1, Z)]
    above = me.at(z=(me.z + 1) % Z)
    below = me.at(z=(me.z + Z - 1) % Z)
    local = []
    for number, (source, target) in enumerate(
        [
            (qw_in, qw),
            (kvw_in, kvw),
            (kvl_in, all_kvl.at[1 + me.y]),
            (ql_in, all_ql.at[me.y]),
            (documents_in, documents),
            (gain_in, gain),
            (ow_in, all_ow.at[me.y]),
        ]
    ):
        copy = pltpu.make_async_copy(source, target, local_sems.at[number])
        copy.start()
        local.append(copy)
    enter([peer, twin, above, below] + fellows)
    for number in (0, 1):
        local[number].wait()
    sends = Sends(send_sems, recv_sems)
    tokens = ql_in.shape[0]
    deep_q, deep_kv = qw.shape[0], kvw.shape[0]
    wide_q, wide_kv = qw.shape[1] // 4, kvw.shape[1] // 4
    depth = att.shape[3]
    rows = out.shape[0] // Z
    mine = pl.ds(pl.multiple_of(me.chip * rows, rows), rows)

    def remote(source, target, send, recv, device):
        return pltpu.make_async_remote_copy(
            source, target, send, recv, device_id=device, device_id_type=MESH
        )

    def slab(array, pair, row, deep):
        return array.at[pair, pl.ds(pl.multiple_of(row * deep, deep), deep)]

    def weight_views(pair):
        def views(origin, part):
            row = origin * 2 + (me.y if part == 0 else 1 - me.y)
            return [slab(all_qw, pair, row, deep_q), slab(all_kvw, pair, row, deep_kv)]

        return views

    def cut(y, pair):
        number = y * 2 + pair
        return [
            qw.at[:, pl.ds(pl.multiple_of(number * wide_q, 128), wide_q)],
            kvw.at[:, pl.ds(pl.multiple_of(number * wide_kv, 128), wide_kv)],
        ]

    def attended_views(pair):
        def views(origin, part):
            return [every.at[pair, origin, me.y if part == 0 else 1 - me.y]]

        return views

    weights = [
        Ring(sends, me, weight_views(pair), [sends.group(), sends.group()]) for pair in range(2)
    ]
    results = [Ring(sends, me, attended_views(pair), [sends.group()]) for pair in range(2)]
    back_groups = [sends.group() for _ in range(2)]
    twin_group, prior_group, lat_q_group, lat_kv_group = (sends.group() for _ in range(4))
    twin_q_group, twin_kv_group, twin_prior_group, out_group = (sends.group() for _ in range(4))
    swaps = [[sends.slot(), sends.slot()] for _ in range(2)]
    backs = [sends.slot() for _ in range(2)]
    twins = [sends.slot() for _ in range(Z)]
    lat_q, lat_kv, twin_q, twin_kv, prior, twin_prior, swap_out = (sends.slot() for _ in range(7))

    def both(ring, steps, part):
        ring.arrive(0, steps, part)
        ring.arrive(1, steps, part)

    def begin(ring, part, sources):
        ring.send(0, 1, part, sources)
        ring.send(1, 1, part, sources)

    def start_weights(pair, part):
        ring = weights[pair]
        if part == 0:
            begin(ring, 0, cut(me.y, pair))
            for number, (source, target) in enumerate(
                zip(cut(me.y, pair), ring.views(me.z, 0))
            ):
                copy = pltpu.make_async_copy(source, target, own_sems.at[2 * pair + number])
                copy.start()
                own.append(copy)
        else:
            for number, target in zip(swaps[pair], ring.views(me.z, 1)):
                sends.arrived(number, target, peer)
            begin(ring, 1, None)

    def swap_weights(pair):
        for group, number, source, target in zip(
            weights[pair].groups, swaps[pair], cut(1 - me.y, pair), weights[pair].views(me.z, 0)
        ):
            sends.start(group, number, source, target, peer)

    def start_results(pair, part):
        ring = results[pair]
        if part == 0:
            sends.start(
                back_groups[pair],
                backs[pair],
                att.at[pair, 1 - me.y],
                every.at[pair, me.z, me.y],
                peer,
            )
            begin(ring, 0, [att.at[pair, me.y]])
        else:
            sends.arrived(backs[pair], every.at[pair, me.z, 1 - me.y], peer)
            begin(ring, 1, None)

    own = []
    half = tokens // 2
    near = pl.ds(pl.multiple_of(me.core * half, half), half)
    far = pl.ds(pl.multiple_of((1 - me.core) * half, half), half)

    def make_tables():
        local[4].wait()
        local[5].wait()
        docs[:, :tokens] = jnp.full((1, tokens), -1.0, jnp.float32)
        docs[:, tokens:] = documents[...].astype(jnp.float32)
        key_docs = docs[:, pl.ds(pl.multiple_of(me.z * 2 * tokens, 128), 3 * tokens)]
        query_docs = jnp.broadcast_to(key_docs[:, tokens:], (128, 2 * tokens)).T
        for block in range(2):
            shape = (tokens, 2 * tokens)
            spot_q = lax.broadcasted_iota(jnp.int32, shape, 0)
            spot_k = lax.broadcasted_iota(jnp.int32, shape, 1)
            same = (
                query_docs[tokens * block : tokens * (block + 1), :1]
                == key_docs[:, tokens * block : tokens * (block + 2)]
            )
            bias[block] = jnp.where(same & (spot_k - tokens <= spot_q), 0.0, -1e30)
        first = me.z * 2 * tokens - tokens
        spots = (first + lax.broadcasted_iota(jnp.int32, (3 * tokens, 128), 0)).astype(jnp.float32)
        angles = spots * inverse[...]
        lane = lax.broadcasted_iota(jnp.int32, (3 * tokens, 128), 1)
        sine = jnp.sin(angles)
        table[...] = jnp.where(
            lane < ROPE, jnp.cos(angles), jnp.where(lane < ROPE + ROPE // 2, -sine, sine)
        )

    def send_latent_kv():
        local[2].wait()
        block = all_kvl.at[1 + me.y, :, near]
        sends.start(lat_kv_group, lat_kv, block, block, peer)

    def send_latent_q():
        local[3].wait()
        block = all_ql.at[me.y, near]
        sends.start(lat_q_group, lat_q, block, block, peer)

    def send_out():
        local[6].wait()
        block = all_ow.at[me.y]
        sends.start(out_group, swap_out, block, block, peer)

    def send_prior():
        block = all_kvl.at[2 - me.y, :, near]
        sends.arrived(lat_kv, block, peer)
        sends.start(
            prior_group, prior, all_kvl.at[2, :, near], all_kvl.at[0, :, near], above
        )
        sends.start(twin_kv_group, twin_kv, block, block, twin)

    def pass_latent_q():
        block = all_ql.at[1 - me.y, near]
        sends.arrived(lat_q, block, peer)
        sends.start(twin_q_group, twin_q, block, block, twin)

    def pass_prior():
        block = all_kvl.at[0, :, near]
        sends.arrived(prior, block, above)
        sends.start(twin_prior_group, twin_prior, block, block, twin)

    def make_keys():
        sends.arrived(twin_kv, all_kvl.at[2 - me.y, :, far], twin)
        sends.arrived(twin_prior, all_kvl.at[0, :, far], twin)
        latents = jnp.concatenate(
            [all_kvl[number].astype(jnp.float32).T for number in range(3)], axis=0
        )
        latent = latents[:, :KL]
        scale = lax.rsqrt(jnp.mean(latent * latent, axis=-1, keepdims=True) + EPSILON)
        normed[...] = (latent * scale * gain[...]).astype(bf16)
        key_rope[...] = turn(latents[:, KL:], table[...]).astype(bf16)

    def make_pair(pair):
        if pair == 0:
            sends.arrived(twin_q, all_ql.at[1 - me.y, far], twin)
        for copy in own[2 * pair : 2 * pair + 2]:
            copy.wait()
        for block in range(2):
            query[tokens * block : tokens * (block + 1), :] = dot(all_ql[block], all_qw[pair])
        key_value[...] = dot(normed[...], all_kvw[pair]).astype(bf16)

    def attend(pair, head):
        start = head * (NOPE + VDIM)
        keys = jnp.concatenate([key_value[:, start : start + NOPE], key_rope[...]], axis=1)
        values = key_value[:, start + NOPE : start + NOPE + VDIM]
        nope = query[:, head * HEAD : head * HEAD + NOPE].astype(bf16)
        rope = turn(query[:, head * HEAD + NOPE : (head + 1) * HEAD], table[tokens:, :])
        queries = jnp.concatenate([nope, rope.astype(bf16)], axis=1)
        for block in range(2):
            window = slice(tokens * block, tokens * (block + 2))
            scores = dot_transposed(queries[tokens * block : tokens * (block + 1)], keys[window])
            scores = scores * (HEAD ** (-0.5)) + bias[block]
            powers = jnp.exp(scores - jnp.max(scores, axis=-1, keepdims=True))
            total = jnp.sum(powers, axis=-1, keepdims=True)
            mixed = dot(powers.astype(bf16), values[window]) * (1.0 / total)
            att[pair, block, :, head * VDIM : (head + 1) * VDIM] = mixed.astype(bf16)

    def product(number, z, which, pairs=(0, 1)):
        total = None
        for y in (me.y, 1 - me.y):
            for pair in pairs:
                if number == 0 and y is me.y:
                    left = att[pair, y]
                else:
                    left = every[pair, z, y]
                part = pl.ds(pl.multiple_of((y * 2 + pair) * depth, depth), depth)
                term = dot_transposed(left, all_ow[which, :, part])
                total = term if total is None else total + term
        return total

    def tile(number):
        z = (me.z + OFFSETS[number]) % Z
        if number == 0:
            sends.arrived(swap_out, all_ow.at[1 - me.y], peer)
        if number == Z - 1:
            ahead[...] = ahead[...] + product(number, z, 1 - me.core, (1,))
            given[number] = ahead[...].astype(bf16)
        else:
            given[number] = product(number, z, 1 - me.core).astype(bf16)
        sends.start(twin_group, twins[number], given.at[number], taken.at[number], twin)
        if number == Z - 1:
            kept[number] = kept[number] + product(number, z, me.core, (1,))
        else:
            kept[number] = product(number, z, me.core)

    def tile_ahead():
        z = (me.z + OFFSETS[Z - 1]) % Z
        ahead[...] = product(Z - 1, z, 1 - me.core, (0,))
        kept[Z - 1] = product(Z - 1, z, me.core, (0,))

    def spread(number):
        sends.arrived(twins[number], taken.at[number], twin)
        summed[number] = (kept[number] + taken[number].astype(jnp.float32)).astype(bf16)
        for step in range(1, Z):
            chip = (me.chip + step) % Z
            part = pl.ds(pl.multiple_of(chip * rows, rows), rows)
            remote(
                summed.at[number, part],
                inbox.at[number, step - 1],
                part_send.at[0],
                part_recv.at[number],
                fellows[step - 1],
            ).start()

    def parts(number):
        return remote(
            inbox.at[number], inbox.at[number], part_send.at[0], part_recv.at[number], peer
        )

    def move(number):
        return remote(
            reduced.at[number],
            moved.at[number],
            move_send.at[0],
            move_recv.at[number],
            me.at(z=(me.z + OFFSETS[number]) % Z),
        )

    def direct():
        return remote(
            reduced.at[Z - 1],
            final.at[mine],
            last.at[0],
            last.at[1],
            me.at(z=(me.z + OFFSETS[Z - 1]) % Z, chip=me.z),
        )

    def finish(number):
        parts(number).wait_recv()
        total = summed[number, mine, :].astype(jnp.float32)
        for source in range(Z - 1):
            total = total + inbox[number, source].astype(jnp.float32)
        if number == 0:
            moved[0] = total.astype(bf16)
        else:
            reduced[number] = total.astype(bf16)
            (direct() if number == Z - 1 else move(number)).start()

    def deliver(number):
        if number:
            move(number).wait_recv()
        chip = (me.z + Z - OFFSETS[number]) % Z

        @pl.when(chip == me.chip)
        def _():
            final[mine, :] = moved[number]

        @pl.when(chip != me.chip)
        def _():
            remote(
                moved.at[number], final.at[mine], last.at[0], last.at[1], me.at(chip=chip)
            ).start()

    swap_weights(0)
    start_weights(0, 0)
    send_latent_kv()
    swap_weights(1)
    send_latent_q()
    start_weights(1, 0)
    start_weights(0, 1)
    weights[0].arrive(1, 1, 0)
    weights[0].arrive(0, 1, 0)
    send_prior()
    weights[0].arrive(1, 1, 1)
    send_out()
    weights[0].arrive(0, 2, 0)
    start_weights(1, 1)
    weights[0].arrive(1, 2, 0)
    make_tables()
    weights[0].arrive(0, 1, 1)
    weights[0].arrive(1, 2, 1)
    weights[1].arrive(1, 1, 0)
    pass_latent_q()
    weights[1].arrive(0, 1, 0)
    weights[0].arrive(0, 3, 0)
    weights[1].arrive(1, 1, 1)
    weights[0].arrive(0, 2, 1)
    weights[1].arrive(0, 2, 0)
    weights[0].arrive(1, 3, 1)
    pass_prior()
    weights[1].arrive(0, 1, 1)
    weights[0].arrive(0, 4, 0)
    weights[1].arrive(1, 2, 1)
    make_keys()
    weights[0].arrive(1, 3, 0)
    weights[1].arrive(1, 2, 0)
    weights[0].arrive(0, 3, 1)
    weights[0].arrive(1, 4, 1)
    make_pair(0)
    weights[1].arrive(0, 3, 0)
    attend(0, 0)
    weights[1].arrive(1, 3, 1)
    attend(0, 1)
    weights[1].arrive(0, 2, 1)
    start_results(0, 0)
    weights[1].arrive(0, 4, 0)
    weights[1].arrive(1, 4, 1)
    weights[1].arrive(1, 3, 0)
    weights[1].arrive(0, 3, 1)
    make_pair(1)
    start_results(0, 1)
    attend(1, 0)
    attend(1, 1)
    start_results(1, 0)
    results[0].arrive(0, 1, 0)
    start_results(1, 1)
    results[1].arrive(1, 1, 0)
    results[1].arrive(0, 1, 0)
    tile(0)
    results[0].arrive(1, 1, 0)
    results[0].arrive(0, 1, 1)
    results[1].arrive(1, 1, 1)
    results[0].arrive(1, 1, 1)
    spread(0)
    results[1].arrive(0, 1, 1)
    tile(2)
    spread(2)
    results[0].arrive(1, 2, 0)
    results[0].arrive(0, 2, 0)
    tile(1)
    results[1].arrive(1, 2, 1)
    results[0].arrive(0, 2, 1)
    results[1].arrive(0, 2, 0)
    spread(1)
    results[1].arrive(0, 2, 1)
    results[0].arrive(1, 2, 1)
    results[1].arrive(1, 2, 0)
    tile(4)
    spread(4)
    tile(3)
    results[1].arrive(0, 3, 0)
    spread(3)
    results[0].arrive(0, 3, 1)
    results[0].arrive(0, 3, 0)
    results[1].arrive(1, 3, 1)
    results[0].arrive(1, 3, 0)
    results[0].arrive(1, 3, 1)
    results[1].arrive(0, 3, 1)
    tile(5)
    finish(4)
    spread(5)
    results[1].arrive(1, 3, 0)
    tile(6)
    finish(1)
    spread(6)
    finish(2)
    results[0].arrive(0, 4, 0)
    results[0].arrive(1, 4, 1)
    tile_ahead()
    results[1].arrive(0, 4, 0)
    results[1].arrive(1, 4, 1)
    tile(7)
    finish(0)
    spread(7)
    finish(6)
    deliver(0)
    finish(3)
    finish(5)
    deliver(1)
    deliver(4)
    deliver(2)
    finish(7)
    deliver(3)
    deliver(6)
    deliver(5)
    for pair in range(2):
        group_q, group_kv = weights[pair].groups
        sends.sent(group_q, all_qw.at[pair, pl.ds(0, 15 * deep_q)], peer)
        sends.sent(group_kv, all_kvw.at[pair, pl.ds(0, 15 * deep_kv)], peer)
        sends.sent(results[pair].groups[0], every.at[pair, pl.ds(0, 7)], peer)
        sends.sent(back_groups[pair], att.at[pair, 0], peer)
    sends.sent(twin_group, given, peer)
    for group, volume in [
        (prior_group, all_kvl.at[0, :, near]),
        (lat_q_group, all_ql.at[0, near]),
        (lat_kv_group, all_kvl.at[0, :, near]),
        (twin_q_group, all_ql.at[0, near]),
        (twin_kv_group, all_kvl.at[0, :, near]),
        (twin_prior_group, all_kvl.at[0, :, near]),
        (out_group, all_ow.at[0]),
    ]:
        sends.sent(group, volume, peer)
    remote(inbox, inbox, part_send.at[0], part_recv.at[0], peer).wait_send()
    moves = moved.at[pl.ds(0, Z - 2)]
    remote(moves, moves, move_send.at[0], move_recv.at[0], peer).wait_send()
    opposite = (me.z - me.chip + Z) % Z == OFFSETS[Z - 1]
    for pick, count in ((opposite, Z), (jnp.logical_not(opposite), Z - 1)):

        @pl.when(pick)
        def _():
            volume = final.at[pl.ds(0, rows * count)]
            remote(volume, volume, last.at[0], last.at[1], peer).wait()

    out[...] = final[...]


def per_device(q_latent, kv_latent, kv_gain, q_weight, kv_weight, out_weight, documents):
    tokens = q_latent.shape[0]
    columns = out_weight.shape[1]
    ctx = lax.axis_size("ctx")
    wide_q, wide_kv = q_weight.shape[1] // 4, kv_weight.shape[1] // 4
    depth = 2 * VDIM
    part = tokens // Z
    bf16, f32 = jnp.bfloat16, jnp.float32
    spot = jnp.arange(128, dtype=f32) % (ROPE // 2)
    inverse = (10000.0 ** (-2.0 * spot / ROPE))[None, :]
    return pl.pallas_call(
        layer_kernel,
        out_shape=jax.ShapeDtypeStruct((tokens, columns), bf16),
        in_specs=[HBM] * 7 + [VM],
        out_specs=VM,
        scratch_shapes=[
            pltpu.VMEM(q_weight.shape, bf16),
            pltpu.VMEM(kv_weight.shape, bf16),
            pltpu.VMEM((1, kv_gain.shape[0]), f32),
            pltpu.VMEM((1, documents.shape[0]), jnp.int32),
            pltpu.VMEM((2, tokens, q_latent.shape[1]), bf16),
            pltpu.VMEM((3, kv_latent.shape[1], tokens), bf16),
            pltpu.VMEM((2, ctx * q_weight.shape[0], wide_q), bf16),
            pltpu.VMEM((2, ctx * kv_weight.shape[0], wide_kv), bf16),
            pltpu.VMEM((2, columns, out_weight.shape[0]), bf16),
            pltpu.VMEM((1, documents.shape[0] + tokens), f32),
            pltpu.VMEM((3 * tokens, 128), f32),
            pltpu.VMEM((2, tokens, 2 * tokens), f32),
            pltpu.VMEM((3 * tokens, KL), bf16),
            pltpu.VMEM((3 * tokens, ROPE), bf16),
            pltpu.VMEM((2 * tokens, wide_q), f32),
            pltpu.VMEM((3 * tokens, wide_kv), bf16),
            pltpu.VMEM((2, 2, tokens, depth), bf16),
            pltpu.VMEM((2, Z, 2, tokens, depth), bf16),
            pltpu.VMEM((Z, tokens, columns), f32),
            pltpu.VMEM((Z, tokens, columns), bf16),
            pltpu.VMEM((Z, tokens, columns), bf16),
            pltpu.VMEM((Z, tokens, columns), bf16),
            pltpu.VMEM((Z, Z - 1, part, columns), bf16),
            pltpu.VMEM((Z, part, columns), bf16),
            pltpu.VMEM((Z, part, columns), bf16),
            pltpu.VMEM((tokens, columns), bf16),
            pltpu.VMEM((tokens, columns), f32),
            pltpu.SemaphoreType.DMA((16,)),
            pltpu.SemaphoreType.DMA((105,)),
            pltpu.SemaphoreType.DMA((7,)),
            pltpu.SemaphoreType.DMA((4,)),
            pltpu.SemaphoreType.DMA((1,)),
            pltpu.SemaphoreType.DMA((Z,)),
            pltpu.SemaphoreType.DMA((1,)),
            pltpu.SemaphoreType.DMA((Z,)),
            pltpu.SemaphoreType.DMA((2,)),
        ],
        compiler_params=pltpu.CompilerParams(
            collective_id=0, has_side_effects=True, vmem_limit_bytes=127 << 19
        ),
        name="layer",
    )(
        q_latent,
        kv_latent.T,
        q_weight,
        kv_weight,
        out_weight.T,
        kv_gain[None, :],
        documents[None, :],
        inverse,
    )


def solution(mesh):
    return jax.shard_map(
        per_device,
        mesh=mesh,
        in_specs=(
            P("ctx", None),
            P("ctx", None),
            P(),
            P("ctx", "grp"),
            P("ctx", "grp"),
            P("grp", "ctx"),
            P(),
        ),
        out_specs=P("ctx", "grp"),
        check_vma=False,
    )
```

```python
import jax
import jax.numpy as jnp
import numpy as np
from jax import lax
from jax.experimental import pallas as pl
from jax.experimental.pallas import tpu as pltpu
from jax.sharding import PartitionSpec as P

KL = 512
NOPE = 128
ROPE = 64
VDIM = 128
HEAD = NOPE + ROPE
Z = 8
MESH = pl.DeviceIdType.MESH
VM = pl.BlockSpec(memory_space=pltpu.VMEM)
HBM = pl.BlockSpec(memory_space=pltpu.HBM)
EPSILON = 1e-06
OFFSETS = [0, 7, 1, 6, 2, 5, 3, 4]


class Place:
    def __init__(self):
        ctx = lax.axis_index("ctx")
        grp = lax.axis_index("grp")
        self.ctx = ctx
        self.z = ctx // 2
        self.y = ctx % 2
        self.chip = grp // 2
        self.core = grp % 2

    def at(self, z=None, y=None, chip=None, core=None):
        z = self.z if z is None else z
        y = self.y if y is None else y
        chip = self.chip if chip is None else chip
        core = self.core if core is None else core
        return (z * 2 + y, chip * 2 + core)


class Sends:
    def __init__(self, send_sems, recv_sems):
        self.send_sems = send_sems
        self.recv_sems = recv_sems
        self.used = 0
        self.groups = 0

    def slot(self):
        self.used += 1
        return self.used - 1

    def group(self):
        self.groups += 1
        return self.groups - 1

    def make(self, group, number, source, target, device):
        return pltpu.make_async_remote_copy(
            source,
            target,
            self.send_sems.at[group],
            self.recv_sems.at[number],
            device_id=device,
            device_id_type=MESH,
        )

    def start(self, group, number, source, target, device):
        self.make(group, number, source, target, device).start()

    def arrived(self, number, target, device):
        self.make(0, number, target, target, device).wait_recv()

    def sent(self, group, volume, device):
        self.make(group, 0, volume, volume, device).wait_send()


def enter(devices):
    barrier = pltpu.get_barrier_semaphore()
    for device in devices:
        pl.semaphore_signal(barrier, inc=1, device_id=device, device_id_type=MESH)
    pl.semaphore_wait(barrier, len(devices))


class Ring:
    def __init__(self, sends, place, views, groups):
        self.sends = sends
        self.groups = groups
        self.place = place
        self.views = views
        self.up = place.at(z=(place.z + 1) % Z)
        self.down = place.at(z=(place.z + Z - 1) % Z)
        self.slots = {}

    def number(self, way, steps, part, which):
        key = (way, steps, part, which)
        if key not in self.slots:
            self.slots[key] = self.sends.slot()
        return self.slots[key]

    def reach(self, way, part):
        return 4 if (way == 0) == (part == 0) else 3

    def send(self, way, steps, part, sources):
        if steps > self.reach(way, part):
            return
        origin = (self.place.z + (Z - steps + 1 if way == 0 else steps - 1)) % Z
        targets = self.views(origin, part)
        for which, (source, target) in enumerate(zip(sources or targets, targets)):
            self.sends.start(
                self.groups[which],
                self.number(way, steps, part, which),
                source,
                target,
                self.up if way == 0 else self.down,
            )

    def arrive(self, way, steps, part):
        if steps > self.reach(way, part):
            return
        origin = (self.place.z + (Z - steps if way == 0 else steps)) % Z
        for which, target in enumerate(self.views(origin, part)):
            self.sends.arrived(self.number(way, steps, part, which), target, self.up)
        self.send(way, steps + 1, part, None)


def dot(left, right):
    return jnp.dot(left, right, preferred_element_type=jnp.float32)


def dot_transposed(left, right):
    return lax.dot_general(
        left, right, (((1,), (1,)), ((), ())), preferred_element_type=jnp.float32
    )


def turn(inputs, table):
    half = ROPE // 2
    swapped = jnp.concatenate([inputs[:, half:], inputs[:, :half]], axis=1)
    return inputs * table[:, :ROPE] + swapped * table[:, ROPE:]


def layer_kernel(
    ql_in,
    kvl_in,
    qw_in,
    kvw_in,
    ow_in,
    gain_in,
    documents_in,
    inverse,
    out,
    qw,
    kvw,
    gain,
    documents,
    all_ql,
    all_kvl,
    all_qw,
    all_kvw,
    all_ow,
    docs,
    table,
    bias,
    normed,
    key_rope,
    query,
    key_value,
    att,
    every,
    kept,
    given,
    taken,
    summed,
    inbox,
    reduced,
    moved,
    final,
    ahead,
    send_sems,
    recv_sems,
    local_sems,
    own_sems,
    part_send,
    part_recv,
    move_send,
    move_recv,
    last,
):
    bf16 = jnp.bfloat16
    me = Place()
    peer = me.at(y=1 - me.y)
    twin = me.at(core=1 - me.core)
    fellows = [me.at(chip=(me.chip + step) % Z) for step in range(1, Z)]
    above = me.at(z=(me.z + 1) % Z)
    below = me.at(z=(me.z + Z - 1) % Z)
    local = []
    for number, (source, target) in enumerate(
        [
            (qw_in, qw),
            (kvw_in, kvw),
            (kvl_in, all_kvl.at[1 + me.y]),
            (ql_in, all_ql.at[me.y]),
            (documents_in, documents),
            (gain_in, gain),
            (ow_in, all_ow.at[me.y]),
        ]
    ):
        copy = pltpu.make_async_copy(source, target, local_sems.at[number])
        copy.start()
        local.append(copy)
    enter([peer, twin, above, below] + fellows)
    for number in (0, 1):
        local[number].wait()
    sends = Sends(send_sems, recv_sems)
    tokens = ql_in.shape[0]
    deep_q, deep_kv = qw.shape[0], kvw.shape[0]
    wide_q, wide_kv = qw.shape[1] // 4, kvw.shape[1] // 4
    depth = att.shape[3]
    rows = out.shape[0] // Z
    mine = pl.ds(pl.multiple_of(me.chip * rows, rows), rows)

    def remote(source, target, send, recv, device):
        return pltpu.make_async_remote_copy(
            source, target, send, recv, device_id=device, device_id_type=MESH
        )

    def slab(array, pair, row, deep):
        return array.at[pair, pl.ds(pl.multiple_of(row * deep, deep), deep)]

    def weight_views(pair):
        def views(origin, part):
            row = origin * 2 + (me.y if part == 0 else 1 - me.y)
            return [slab(all_qw, pair, row, deep_q), slab(all_kvw, pair, row, deep_kv)]

        return views

    def cut(y, pair):
        number = y * 2 + pair
        return [
            qw.at[:, pl.ds(pl.multiple_of(number * wide_q, 128), wide_q)],
            kvw.at[:, pl.ds(pl.multiple_of(number * wide_kv, 128), wide_kv)],
        ]

    def attended_views(pair):
        def views(origin, part):
            return [every.at[pair, origin, me.y if part == 0 else 1 - me.y]]

        return views

    weights = [
        Ring(sends, me, weight_views(pair), [sends.group(), sends.group()]) for pair in range(2)
    ]
    results = [Ring(sends, me, attended_views(pair), [sends.group()]) for pair in range(2)]
    back_groups = [sends.group() for _ in range(2)]
    twin_group, prior_group, lat_q_group, lat_kv_group = (sends.group() for _ in range(4))
    twin_q_group, twin_kv_group, twin_prior_group, out_group = (sends.group() for _ in range(4))
    swaps = [[sends.slot(), sends.slot()] for _ in range(2)]
    backs = [sends.slot() for _ in range(2)]
    twins = [sends.slot() for _ in range(Z)]
    lat_q, lat_kv, twin_q, twin_kv, prior, twin_prior, swap_out = (sends.slot() for _ in range(7))

    def both(ring, steps, part):
        ring.arrive(0, steps, part)
        ring.arrive(1, steps, part)

    def begin(ring, part, sources):
        ring.send(0, 1, part, sources)
        ring.send(1, 1, part, sources)

    def start_weights(pair, part):
        ring = weights[pair]
        if part == 0:
            begin(ring, 0, cut(me.y, pair))
            for number, (source, target) in enumerate(
                zip(cut(me.y, pair), ring.views(me.z, 0))
            ):
                copy = pltpu.make_async_copy(source, target, own_sems.at[2 * pair + number])
                copy.start()
                own.append(copy)
        else:
            for number, target in zip(swaps[pair], ring.views(me.z, 1)):
                sends.arrived(number, target, peer)
            begin(ring, 1, None)

    def swap_weights(pair):
        for group, number, source, target in zip(
            weights[pair].groups, swaps[pair], cut(1 - me.y, pair), weights[pair].views(me.z, 0)
        ):
            sends.start(group, number, source, target, peer)

    def start_results(pair, part):
        ring = results[pair]
        if part == 0:
            sends.start(
                back_groups[pair],
                backs[pair],
                att.at[pair, 1 - me.y],
                every.at[pair, me.z, me.y],
                peer,
            )
            begin(ring, 0, [att.at[pair, me.y]])
        else:
            sends.arrived(backs[pair], every.at[pair, me.z, 1 - me.y], peer)
            begin(ring, 1, None)

    own = []
    half = tokens // 2
    near = pl.ds(pl.multiple_of(me.core * half, half), half)
    far = pl.ds(pl.multiple_of((1 - me.core) * half, half), half)

    def make_tables():
        local[4].wait()
        local[5].wait()
        docs[:, :tokens] = jnp.full((1, tokens), -1.0, jnp.float32)
        docs[:, tokens:] = documents[...].astype(jnp.float32)
        key_docs = docs[:, pl.ds(pl.multiple_of(me.z * 2 * tokens, 128), 3 * tokens)]
        query_docs = jnp.broadcast_to(key_docs[:, tokens:], (128, 2 * tokens)).T
        for block in range(2):
            shape = (tokens, 2 * tokens)
            spot_q = lax.broadcasted_iota(jnp.int32, shape, 0)
            spot_k = lax.broadcasted_iota(jnp.int32, shape, 1)
            same = (
                query_docs[tokens * block : tokens * (block + 1), :1]
                == key_docs[:, tokens * block : tokens * (block + 2)]
            )
            bias[block] = jnp.where(same & (spot_k - tokens <= spot_q), 0.0, -1e30)
        first = me.z * 2 * tokens - tokens
        spots = (first + lax.broadcasted_iota(jnp.int32, (3 * tokens, 128), 0)).astype(jnp.float32)
        angles = spots * inverse[...]
        lane = lax.broadcasted_iota(jnp.int32, (3 * tokens, 128), 1)
        sine = jnp.sin(angles)
        table[...] = jnp.where(
            lane < ROPE, jnp.cos(angles), jnp.where(lane < ROPE + ROPE // 2, -sine, sine)
        )

    def send_latent_kv():
        local[2].wait()
        block = all_kvl.at[1 + me.y, :, near]
        sends.start(lat_kv_group, lat_kv, block, block, peer)

    def send_latent_q():
        local[3].wait()
        block = all_ql.at[me.y, near]
        sends.start(lat_q_group, lat_q, block, block, peer)

    def send_out():
        local[6].wait()
        block = all_ow.at[me.y]
        sends.start(out_group, swap_out, block, block, peer)

    def send_prior():
        block = all_kvl.at[2 - me.y, :, near]
        sends.arrived(lat_kv, block, peer)
        sends.start(
            prior_group, prior, all_kvl.at[2, :, near], all_kvl.at[0, :, near], above
        )
        sends.start(twin_kv_group, twin_kv, block, block, twin)

    def pass_latent_q():
        block = all_ql.at[1 - me.y, near]
        sends.arrived(lat_q, block, peer)
        sends.start(twin_q_group, twin_q, block, block, twin)

    def pass_prior():
        block = all_kvl.at[0, :, near]
        sends.arrived(prior, block, above)
        sends.start(twin_prior_group, twin_prior, block, block, twin)

    def make_keys():
        sends.arrived(twin_kv, all_kvl.at[2 - me.y, :, far], twin)
        sends.arrived(twin_prior, all_kvl.at[0, :, far], twin)
        latents = jnp.concatenate(
            [all_kvl[number].astype(jnp.float32).T for number in range(3)], axis=0
        )
        latent = latents[:, :KL]
        scale = lax.rsqrt(jnp.mean(latent * latent, axis=-1, keepdims=True) + EPSILON)
        normed[...] = (latent * scale * gain[...]).astype(bf16)
        key_rope[...] = turn(latents[:, KL:], table[...]).astype(bf16)

    def make_pair(pair):
        if pair == 0:
            sends.arrived(twin_q, all_ql.at[1 - me.y, far], twin)
        for copy in own[2 * pair : 2 * pair + 2]:
            copy.wait()
        for block in range(2):
            query[tokens * block : tokens * (block + 1), :] = dot(all_ql[block], all_qw[pair])
        key_value[...] = dot(normed[...], all_kvw[pair]).astype(bf16)

    def attend(pair, head):
        start = head * (NOPE + VDIM)
        keys = jnp.concatenate([key_value[:, start : start + NOPE], key_rope[...]], axis=1)
        values = key_value[:, start + NOPE : start + NOPE + VDIM]
        nope = query[:, head * HEAD : head * HEAD + NOPE].astype(bf16)
        rope = turn(query[:, head * HEAD + NOPE : (head + 1) * HEAD], table[tokens:, :])
        queries = jnp.concatenate([nope, rope.astype(bf16)], axis=1)
        for block in range(2):
            window = slice(tokens * block, tokens * (block + 2))
            scores = dot_transposed(queries[tokens * block : tokens * (block + 1)], keys[window])
            scores = scores * (HEAD ** (-0.5)) + bias[block]
            powers = jnp.exp(scores - jnp.max(scores, axis=-1, keepdims=True))
            total = jnp.sum(powers, axis=-1, keepdims=True)
            mixed = dot(powers.astype(bf16), values[window]) * (1.0 / total)
            att[pair, block, :, head * VDIM : (head + 1) * VDIM] = mixed.astype(bf16)

    def product(number, z, which, pairs=(0, 1)):
        total = None
        for y in (me.y, 1 - me.y):
            for pair in pairs:
                if number == 0 and y is me.y:
                    left = att[pair, y]
                else:
                    left = every[pair, z, y]
                part = pl.ds(pl.multiple_of((y * 2 + pair) * depth, depth), depth)
                term = dot_transposed(left, all_ow[which, :, part])
                total = term if total is None else total + term
        return total

    def tile(number):
        z = (me.z + OFFSETS[number]) % Z
        if number == 0:
            sends.arrived(swap_out, all_ow.at[1 - me.y], peer)
        if number == Z - 1:
            ahead[...] = ahead[...] + product(number, z, 1 - me.core, (1,))
            given[number] = ahead[...].astype(bf16)
        else:
            given[number] = product(number, z, 1 - me.core).astype(bf16)
        sends.start(twin_group, twins[number], given.at[number], taken.at[number], twin)
        if number == Z - 1:
            kept[number] = kept[number] + product(number, z, me.core, (1,))
        else:
            kept[number] = product(number, z, me.core)

    def tile_ahead():
        z = (me.z + OFFSETS[Z - 1]) % Z
        ahead[...] = product(Z - 1, z, 1 - me.core, (0,))
        kept[Z - 1] = product(Z - 1, z, me.core, (0,))

    def spread(number):
        sends.arrived(twins[number], taken.at[number], twin)
        summed[number] = (kept[number] + taken[number].astype(jnp.float32)).astype(bf16)
        for step in range(1, Z):
            chip = (me.chip + step) % Z
            part = pl.ds(pl.multiple_of(chip * rows, rows), rows)
            remote(
                summed.at[number, part],
                inbox.at[number, step - 1],
                part_send.at[0],
                part_recv.at[number],
                fellows[step - 1],
            ).start()

    def parts(number):
        return remote(
            inbox.at[number], inbox.at[number], part_send.at[0], part_recv.at[number], peer
        )

    def move(number):
        return remote(
            reduced.at[number],
            moved.at[number],
            move_send.at[0],
            move_recv.at[number],
            me.at(z=(me.z + OFFSETS[number]) % Z),
        )

    def direct():
        return remote(
            reduced.at[Z - 1],
            final.at[mine],
            last.at[0],
            last.at[1],
            me.at(z=(me.z + OFFSETS[Z - 1]) % Z, chip=me.z),
        )

    def finish(number):
        parts(number).wait_recv()
        total = summed[number, mine, :].astype(jnp.float32)
        for source in range(Z - 1):
            total = total + inbox[number, source].astype(jnp.float32)
        if number == 0:
            moved[0] = total.astype(bf16)
        else:
            reduced[number] = total.astype(bf16)
            (direct() if number == Z - 1 else move(number)).start()

    def deliver(number):
        if number:
            move(number).wait_recv()
        chip = (me.z + Z - OFFSETS[number]) % Z

        @pl.when(chip == me.chip)
        def _():
            final[mine, :] = moved[number]

        @pl.when(chip != me.chip)
        def _():
            remote(
                moved.at[number], final.at[mine], last.at[0], last.at[1], me.at(chip=chip)
            ).start()

    start_weights(0, 0)
    swap_weights(0)
    start_weights(1, 0)
    swap_weights(1)
    send_latent_kv()
    make_tables()
    send_latent_q()
    weights[0].arrive(0, 1, 0)
    start_weights(0, 1)
    weights[0].arrive(1, 1, 0)
    weights[1].arrive(0, 1, 0)
    start_weights(1, 1)
    weights[0].arrive(0, 2, 0)
    weights[0].arrive(1, 2, 0)
    send_out()
    weights[0].arrive(1, 1, 1)
    weights[0].arrive(0, 1, 1)
    send_prior()
    weights[1].arrive(1, 1, 1)
    weights[0].arrive(1, 2, 1)
    weights[1].arrive(0, 1, 1)
    weights[1].arrive(1, 1, 0)
    weights[0].arrive(0, 3, 0)
    weights[1].arrive(0, 2, 0)
    pass_prior()
    pass_latent_q()
    weights[1].arrive(1, 2, 1)
    make_keys()
    weights[0].arrive(1, 3, 1)
    weights[1].arrive(1, 2, 0)
    weights[0].arrive(0, 2, 1)
    weights[1].arrive(1, 3, 1)
    weights[1].arrive(0, 2, 1)
    weights[0].arrive(0, 4, 0)
    weights[0].arrive(1, 3, 0)
    weights[1].arrive(0, 3, 0)
    weights[0].arrive(1, 4, 1)
    weights[0].arrive(0, 3, 1)
    make_pair(0)
    attend(0, 0)
    weights[1].arrive(0, 3, 1)
    attend(0, 1)
    weights[1].arrive(1, 3, 0)
    weights[1].arrive(1, 4, 1)
    start_results(0, 0)
    weights[1].arrive(0, 4, 0)
    make_pair(1)
    attend(1, 0)
    attend(1, 1)
    start_results(1, 0)
    results[0].arrive(1, 1, 0)
    results[0].arrive(0, 1, 0)
    start_results(0, 1)
    start_results(1, 1)
    tile(0)
    results[1].arrive(1, 1, 0)
    results[0].arrive(0, 1, 1)
    results[1].arrive(0, 1, 1)
    results[0].arrive(1, 1, 1)
    results[1].arrive(0, 1, 0)
    spread(0)
    results[1].arrive(1, 1, 1)
    tile(2)
    results[1].arrive(1, 2, 0)
    tile(1)
    results[0].arrive(0, 2, 0)
    spread(2)
    results[0].arrive(1, 2, 1)
    results[0].arrive(1, 2, 0)
    finish(0)
    results[1].arrive(0, 2, 0)
    results[1].arrive(1, 2, 1)
    results[0].arrive(0, 2, 1)
    results[1].arrive(0, 2, 1)
    spread(1)
    tile(4)
    spread(4)
    results[1].arrive(1, 3, 0)
    tile(3)
    results[0].arrive(0, 3, 1)
    spread(3)
    results[0].arrive(0, 3, 0)
    results[1].arrive(0, 3, 0)
    results[0].arrive(1, 3, 1)
    finish(1)
    results[1].arrive(0, 3, 1)
    tile(5)
    results[1].arrive(1, 3, 1)
    results[0].arrive(1, 3, 0)
    spread(5)
    tile(6)
    finish(2)
    results[0].arrive(1, 4, 1)
    spread(6)
    results[0].arrive(0, 4, 0)
    finish(4)
    results[1].arrive(0, 4, 0)
    deliver(0)
    tile_ahead()
    results[1].arrive(1, 4, 1)
    tile(7)
    spread(7)
    finish(5)
    deliver(1)
    finish(6)
    finish(3)
    deliver(5)
    deliver(2)
    finish(7)
    deliver(4)
    deliver(6)
    deliver(3)
    for pair in range(2):
        group_q, group_kv = weights[pair].groups
        sends.sent(group_q, all_qw.at[pair, pl.ds(0, 15 * deep_q)], peer)
        sends.sent(group_kv, all_kvw.at[pair, pl.ds(0, 15 * deep_kv)], peer)
        sends.sent(results[pair].groups[0], every.at[pair, pl.ds(0, 7)], peer)
        sends.sent(back_groups[pair], att.at[pair, 0], peer)
    sends.sent(twin_group, given, peer)
    for group, volume in [
        (prior_group, all_kvl.at[0, :, near]),
        (lat_q_group, all_ql.at[0, near]),
        (lat_kv_group, all_kvl.at[0, :, near]),
        (twin_q_group, all_ql.at[0, near]),
        (twin_kv_group, all_kvl.at[0, :, near]),
        (twin_prior_group, all_kvl.at[0, :, near]),
        (out_group, all_ow.at[0]),
    ]:
        sends.sent(group, volume, peer)
    remote(inbox, inbox, part_send.at[0], part_recv.at[0], peer).wait_send()
    moves = moved.at[pl.ds(0, Z - 2)]
    remote(moves, moves, move_send.at[0], move_recv.at[0], peer).wait_send()
    opposite = (me.z - me.chip + Z) % Z == OFFSETS[Z - 1]
    for pick, count in ((opposite, Z), (jnp.logical_not(opposite), Z - 1)):

        @pl.when(pick)
        def _():
            volume = final.at[pl.ds(0, rows * count)]
            remote(volume, volume, last.at[0], last.at[1], peer).wait()

    out[...] = final[...]


def per_device(q_latent, kv_latent, kv_gain, q_weight, kv_weight, out_weight, documents):
    tokens = q_latent.shape[0]
    columns = out_weight.shape[1]
    ctx = lax.axis_size("ctx")
    wide_q, wide_kv = q_weight.shape[1] // 4, kv_weight.shape[1] // 4
    depth = 2 * VDIM
    part = tokens // Z
    bf16, f32 = jnp.bfloat16, jnp.float32
    spot = np.arange(128) % (ROPE // 2)
    inverse = (10000.0 ** (-2.0 * spot / ROPE)).astype(np.float32)[None, :]
    return pl.pallas_call(
        layer_kernel,
        out_shape=pltpu.VMEM((tokens, columns), bf16),
        in_specs=[HBM] * 7 + [VM],
        out_specs=VM,
        scratch_shapes=[
            pltpu.VMEM(q_weight.shape, bf16),
            pltpu.VMEM(kv_weight.shape, bf16),
            pltpu.VMEM((1, kv_gain.shape[0]), f32),
            pltpu.VMEM((1, documents.shape[0]), jnp.int32),
            pltpu.VMEM((2, tokens, q_latent.shape[1]), bf16),
            pltpu.VMEM((3, kv_latent.shape[1], tokens), bf16),
            pltpu.VMEM((2, ctx * q_weight.shape[0], wide_q), bf16),
            pltpu.VMEM((2, ctx * kv_weight.shape[0], wide_kv), bf16),
            pltpu.VMEM((2, columns, out_weight.shape[0]), bf16),
            pltpu.VMEM((1, documents.shape[0] + tokens), f32),
            pltpu.VMEM((3 * tokens, 128), f32),
            pltpu.VMEM((2, tokens, 2 * tokens), f32),
            pltpu.VMEM((3 * tokens, KL), bf16),
            pltpu.VMEM((3 * tokens, ROPE), bf16),
            pltpu.VMEM((2 * tokens, wide_q), f32),
            pltpu.VMEM((3 * tokens, wide_kv), bf16),
            pltpu.VMEM((2, 2, tokens, depth), bf16),
            pltpu.VMEM((2, Z, 2, tokens, depth), bf16),
            pltpu.VMEM((Z, tokens, columns), f32),
            pltpu.VMEM((Z, tokens, columns), bf16),
            pltpu.VMEM((Z, tokens, columns), bf16),
            pltpu.VMEM((Z, tokens, columns), bf16),
            pltpu.VMEM((Z, Z - 1, part, columns), bf16),
            pltpu.VMEM((Z, part, columns), bf16),
            pltpu.VMEM((Z, part, columns), bf16),
            pltpu.VMEM((tokens, columns), bf16),
            pltpu.VMEM((tokens, columns), f32),
            pltpu.SemaphoreType.DMA((16,)),
            pltpu.SemaphoreType.DMA((105,)),
            pltpu.SemaphoreType.DMA((7,)),
            pltpu.SemaphoreType.DMA((4,)),
            pltpu.SemaphoreType.DMA((1,)),
            pltpu.SemaphoreType.DMA((Z,)),
            pltpu.SemaphoreType.DMA((1,)),
            pltpu.SemaphoreType.DMA((Z,)),
            pltpu.SemaphoreType.DMA((2,)),
        ],
        compiler_params=pltpu.CompilerParams(
            collective_id=0, has_side_effects=True, vmem_limit_bytes=62 << 20
        ),
        name="layer",
    )(
        q_latent,
        kv_latent.T,
        q_weight,
        kv_weight,
        out_weight.T,
        kv_gain[None, :],
        documents[None, :],
        inverse,
    )


def solution(mesh):
    return jax.shard_map(
        per_device,
        mesh=mesh,
        in_specs=(
            P("ctx", None),
            P("ctx", None),
            P(),
            P("ctx", "grp"),
            P("ctx", "grp"),
            P("grp", "ctx"),
            P(),
        ),
        out_specs=P("ctx", "grp"),
        check_vma=False,
    )
```

```python
import jax
import jax.numpy as jnp
import numpy as np
from jax import lax
from jax.experimental import pallas as pl
from jax.experimental.pallas import tpu as pltpu
from jax.sharding import PartitionSpec as P

KL = 512
NOPE = 128
ROPE = 64
VDIM = 128
HEAD = NOPE + ROPE
Z = 8
MESH = pl.DeviceIdType.MESH
VM = pl.BlockSpec(memory_space=pltpu.VMEM)
HBM = pl.BlockSpec(memory_space=pltpu.HBM)
EPSILON = 1e-06
OFFSETS = [0, 7, 1, 6, 2, 5, 3, 4]


class Place:
    def __init__(self):
        ctx = lax.axis_index("ctx")
        grp = lax.axis_index("grp")
        self.ctx = ctx
        self.z = ctx // 2
        self.y = ctx % 2
        self.chip = grp // 2
        self.core = grp % 2

    def at(self, z=None, y=None, chip=None, core=None):
        z = self.z if z is None else z
        y = self.y if y is None else y
        chip = self.chip if chip is None else chip
        core = self.core if core is None else core
        return (z * 2 + y, chip * 2 + core)


class Sends:
    def __init__(self, send_sems, recv_sems):
        self.send_sems = send_sems
        self.recv_sems = recv_sems
        self.used = 0
        self.groups = 0

    def slot(self):
        self.used += 1
        return self.used - 1

    def group(self):
        self.groups += 1
        return self.groups - 1

    def make(self, group, number, source, target, device):
        return pltpu.make_async_remote_copy(
            source,
            target,
            self.send_sems.at[group],
            self.recv_sems.at[number],
            device_id=device,
            device_id_type=MESH,
        )

    def start(self, group, number, source, target, device):
        self.make(group, number, source, target, device).start()

    def arrived(self, number, target, device):
        self.make(0, number, target, target, device).wait_recv()

    def sent(self, group, volume, device):
        self.make(group, 0, volume, volume, device).wait_send()


def enter(devices):
    barrier = pltpu.get_barrier_semaphore()
    for device in devices:
        pl.semaphore_signal(barrier, inc=1, device_id=device, device_id_type=MESH)
    pl.semaphore_wait(barrier, len(devices))


class Ring:
    def __init__(self, sends, place, views, groups):
        self.sends = sends
        self.groups = groups
        self.place = place
        self.views = views
        self.up = place.at(z=(place.z + 1) % Z)
        self.down = place.at(z=(place.z + Z - 1) % Z)
        self.slots = {}

    def number(self, way, steps, part, which):
        key = (way, steps, part, which)
        if key not in self.slots:
            self.slots[key] = self.sends.slot()
        return self.slots[key]

    def reach(self, way, part):
        return 4 if (way == 0) == (part == 0) else 3

    def send(self, way, steps, part, sources):
        if steps > self.reach(way, part):
            return
        origin = (self.place.z + (Z - steps + 1 if way == 0 else steps - 1)) % Z
        targets = self.views(origin, part)
        for which, (source, target) in enumerate(zip(sources or targets, targets)):
            self.sends.start(
                self.groups[which],
                self.number(way, steps, part, which),
                source,
                target,
                self.up if way == 0 else self.down,
            )

    def arrive(self, way, steps, part):
        if steps > self.reach(way, part):
            return
        origin = (self.place.z + (Z - steps if way == 0 else steps)) % Z
        for which, target in enumerate(self.views(origin, part)):
            self.sends.arrived(self.number(way, steps, part, which), target, self.up)
        self.send(way, steps + 1, part, None)


def dot(left, right):
    return jnp.dot(left, right, preferred_element_type=jnp.float32)


def dot_transposed(left, right):
    return lax.dot_general(
        left, right, (((1,), (1,)), ((), ())), preferred_element_type=jnp.float32
    )


def turn(inputs, table):
    half = ROPE // 2
    swapped = jnp.concatenate([inputs[:, half:], inputs[:, :half]], axis=1)
    return inputs * table[:, :ROPE] + swapped * table[:, ROPE:]


def layer_kernel(
    ql_in,
    kvl_in,
    qw_in,
    kvw_in,
    ow_in,
    gain_in,
    documents_in,
    inverse,
    out,
    qw,
    kvw,
    gain,
    documents,
    all_ql,
    all_kvl,
    all_qw,
    all_kvw,
    all_ow,
    docs,
    table,
    bias,
    normed,
    key_rope,
    query,
    key_value,
    att,
    every,
    kept,
    given,
    taken,
    summed,
    inbox,
    reduced,
    moved,
    final,
    ahead,
    send_sems,
    recv_sems,
    local_sems,
    own_sems,
    part_send,
    part_recv,
    move_send,
    move_recv,
    last,
):
    bf16 = jnp.bfloat16
    me = Place()
    peer = me.at(y=1 - me.y)
    twin = me.at(core=1 - me.core)
    fellows = [me.at(chip=(me.chip + step) % Z) for step in range(1, Z)]
    above = me.at(z=(me.z + 1) % Z)
    below = me.at(z=(me.z + Z - 1) % Z)
    local = []
    for number, (source, target) in enumerate(
        [
            (qw_in, qw),
            (kvw_in, kvw),
            (kvl_in, all_kvl.at[1 + me.y]),
            (ql_in, all_ql.at[me.y]),
            (documents_in, documents),
            (gain_in, gain),
            (ow_in, all_ow.at[me.y]),
        ]
    ):
        copy = pltpu.make_async_copy(source, target, local_sems.at[number])
        copy.start()
        local.append(copy)
    enter([peer, twin, above, below] + fellows)
    for number in (0, 1):
        local[number].wait()
    sends = Sends(send_sems, recv_sems)
    tokens = ql_in.shape[0]
    deep_q, deep_kv = qw.shape[0], kvw.shape[0]
    wide_q, wide_kv = qw.shape[1] // 4, kvw.shape[1] // 4
    depth = att.shape[3]
    rows = out.shape[0] // Z
    mine = pl.ds(pl.multiple_of(me.chip * rows, rows), rows)

    def remote(source, target, send, recv, device):
        return pltpu.make_async_remote_copy(
            source, target, send, recv, device_id=device, device_id_type=MESH
        )

    def slab(array, pair, row, deep):
        return array.at[pair, pl.ds(pl.multiple_of(row * deep, deep), deep)]

    def weight_views(pair):
        def views(origin, part):
            row = origin * 2 + (me.y if part == 0 else 1 - me.y)
            return [slab(all_qw, pair, row, deep_q), slab(all_kvw, pair, row, deep_kv)]

        return views

    def cut(y, pair):
        number = y * 2 + pair
        return [
            qw.at[:, pl.ds(pl.multiple_of(number * wide_q, 128), wide_q)],
            kvw.at[:, pl.ds(pl.multiple_of(number * wide_kv, 128), wide_kv)],
        ]

    def attended_views(pair):
        def views(origin, part):
            return [every.at[pair, origin, me.y if part == 0 else 1 - me.y]]

        return views

    weights = [
        Ring(sends, me, weight_views(pair), [sends.group(), sends.group()]) for pair in range(2)
    ]
    results = [Ring(sends, me, attended_views(pair), [sends.group()]) for pair in range(2)]
    back_groups = [sends.group() for _ in range(2)]
    twin_group, prior_group, lat_q_group, lat_kv_group = (sends.group() for _ in range(4))
    twin_q_group, twin_kv_group, twin_prior_group, out_group = (sends.group() for _ in range(4))
    swaps = [[sends.slot(), sends.slot()] for _ in range(2)]
    backs = [sends.slot() for _ in range(2)]
    twins = [sends.slot() for _ in range(Z)]
    lat_q, lat_kv, twin_q, twin_kv, prior, twin_prior, swap_out = (sends.slot() for _ in range(7))

    def both(ring, steps, part):
        ring.arrive(0, steps, part)
        ring.arrive(1, steps, part)

    def begin(ring, part, sources):
        ring.send(0, 1, part, sources)
        ring.send(1, 1, part, sources)

    def start_weights(pair, part):
        ring = weights[pair]
        if part == 0:
            begin(ring, 0, cut(me.y, pair))
            for number, (source, target) in enumerate(
                zip(cut(me.y, pair), ring.views(me.z, 0))
            ):
                copy = pltpu.make_async_copy(source, target, own_sems.at[2 * pair + number])
                copy.start()
                own.append(copy)
        else:
            for number, target in zip(swaps[pair], ring.views(me.z, 1)):
                sends.arrived(number, target, peer)
            begin(ring, 1, None)

    def swap_weights(pair):
        for group, number, source, target in zip(
            weights[pair].groups, swaps[pair], cut(1 - me.y, pair), weights[pair].views(me.z, 0)
        ):
            sends.start(group, number, source, target, peer)

    def start_results(pair, part):
        ring = results[pair]
        if part == 0:
            sends.start(
                back_groups[pair],
                backs[pair],
                att.at[pair, 1 - me.y],
                every.at[pair, me.z, me.y],
                peer,
            )
            begin(ring, 0, [att.at[pair, me.y]])
        else:
            sends.arrived(backs[pair], every.at[pair, me.z, 1 - me.y], peer)
            begin(ring, 1, None)

    own = []
    half = tokens // 2
    near = pl.ds(pl.multiple_of(me.core * half, half), half)
    far = pl.ds(pl.multiple_of((1 - me.core) * half, half), half)

    def make_tables():
        local[4].wait()
        local[5].wait()
        docs[:, :tokens] = jnp.full((1, tokens), -1.0, jnp.float32)
        docs[:, tokens:] = documents[...].astype(jnp.float32)
        key_docs = docs[:, pl.ds(pl.multiple_of(me.z * 2 * tokens, 128), 3 * tokens)]
        query_docs = jnp.broadcast_to(key_docs[:, tokens:], (128, 2 * tokens)).T
        for block in range(2):
            shape = (tokens, 2 * tokens)
            spot_q = lax.broadcasted_iota(jnp.int32, shape, 0)
            spot_k = lax.broadcasted_iota(jnp.int32, shape, 1)
            same = (
                query_docs[tokens * block : tokens * (block + 1), :1]
                == key_docs[:, tokens * block : tokens * (block + 2)]
            )
            bias[block] = jnp.where(same & (spot_k - tokens <= spot_q), 0.0, -1e30)
        first = me.z * 2 * tokens - tokens
        spots = (first + lax.broadcasted_iota(jnp.int32, (3 * tokens, 128), 0)).astype(jnp.float32)
        angles = spots * inverse[...]
        lane = lax.broadcasted_iota(jnp.int32, (3 * tokens, 128), 1)
        sine = jnp.sin(angles)
        table[...] = jnp.where(
            lane < ROPE, jnp.cos(angles), jnp.where(lane < ROPE + ROPE // 2, -sine, sine)
        )

    def send_latent_kv():
        local[2].wait()
        block = all_kvl.at[1 + me.y, :, near]
        sends.start(lat_kv_group, lat_kv, block, block, peer)

    def send_latent_q():
        local[3].wait()
        block = all_ql.at[me.y, near]
        sends.start(lat_q_group, lat_q, block, block, peer)

    def send_out():
        local[6].wait()
        block = all_ow.at[me.y]
        sends.start(out_group, swap_out, block, block, peer)

    def send_prior():
        block = all_kvl.at[2 - me.y, :, near]
        sends.arrived(lat_kv, block, peer)
        sends.start(
            prior_group, prior, all_kvl.at[2, :, near], all_kvl.at[0, :, near], above
        )
        sends.start(twin_kv_group, twin_kv, block, block, twin)

    def pass_latent_q():
        block = all_ql.at[1 - me.y, near]
        sends.arrived(lat_q, block, peer)
        sends.start(twin_q_group, twin_q, block, block, twin)

    def pass_prior():
        block = all_kvl.at[0, :, near]
        sends.arrived(prior, block, above)
        sends.start(twin_prior_group, twin_prior, block, block, twin)

    def make_keys():
        sends.arrived(twin_kv, all_kvl.at[2 - me.y, :, far], twin)
        sends.arrived(twin_prior, all_kvl.at[0, :, far], twin)
        latents = jnp.concatenate(
            [all_kvl[number].astype(jnp.float32).T for number in range(3)], axis=0
        )
        latent = latents[:, :KL]
        scale = lax.rsqrt(jnp.mean(latent * latent, axis=-1, keepdims=True) + EPSILON)
        normed[...] = (latent * scale * gain[...]).astype(bf16)
        key_rope[...] = turn(latents[:, KL:], table[...]).astype(bf16)

    def make_pair(pair):
        if pair == 0:
            sends.arrived(twin_q, all_ql.at[1 - me.y, far], twin)
        for copy in own[2 * pair : 2 * pair + 2]:
            copy.wait()
        for block in range(2):
            query[tokens * block : tokens * (block + 1), :] = dot(all_ql[block], all_qw[pair])
        key_value[...] = dot(normed[...], all_kvw[pair]).astype(bf16)

    def attend(pair, head):
        start = head * (NOPE + VDIM)
        keys = jnp.concatenate([key_value[:, start : start + NOPE], key_rope[...]], axis=1)
        values = key_value[:, start + NOPE : start + NOPE + VDIM]
        nope = query[:, head * HEAD : head * HEAD + NOPE].astype(bf16)
        rope = turn(query[:, head * HEAD + NOPE : (head + 1) * HEAD], table[tokens:, :])
        queries = jnp.concatenate([nope, rope.astype(bf16)], axis=1)
        for block in range(2):
            window = slice(tokens * block, tokens * (block + 2))
            scores = dot_transposed(queries[tokens * block : tokens * (block + 1)], keys[window])
            scores = scores * (HEAD ** (-0.5)) + bias[block]
            powers = jnp.exp(scores - jnp.max(scores, axis=-1, keepdims=True))
            total = jnp.sum(powers, axis=-1, keepdims=True)
            mixed = dot(powers.astype(bf16), values[window]) * (1.0 / total)
            att[pair, block, :, head * VDIM : (head + 1) * VDIM] = mixed.astype(bf16)

    def product(number, z, which, pairs=(0, 1)):
        total = None
        for y in (me.y, 1 - me.y):
            for pair in pairs:
                if number == 0 and y is me.y:
                    left = att[pair, y]
                else:
                    left = every[pair, z, y]
                part = pl.ds(pl.multiple_of((y * 2 + pair) * depth, depth), depth)
                term = dot_transposed(left, all_ow[which, :, part])
                total = term if total is None else total + term
        return total

    def tile(number):
        z = (me.z + OFFSETS[number]) % Z
        if number == 0:
            sends.arrived(swap_out, all_ow.at[1 - me.y], peer)
        if number == Z - 1:
            ahead[...] = ahead[...] + product(number, z, 1 - me.core, (1,))
            given[number] = ahead[...].astype(bf16)
        else:
            given[number] = product(number, z, 1 - me.core).astype(bf16)
        sends.start(twin_group, twins[number], given.at[number], taken.at[number], twin)
        if number == Z - 1:
            kept[number] = kept[number] + product(number, z, me.core, (1,))
        else:
            kept[number] = product(number, z, me.core)

    def tile_ahead():
        z = (me.z + OFFSETS[Z - 1]) % Z
        ahead[...] = product(Z - 1, z, 1 - me.core, (0,))
        kept[Z - 1] = product(Z - 1, z, me.core, (0,))

    def spread(number):
        sends.arrived(twins[number], taken.at[number], twin)
        summed[number] = (kept[number] + taken[number].astype(jnp.float32)).astype(bf16)
        for step in range(1, Z):
            chip = (me.chip + step) % Z
            part = pl.ds(pl.multiple_of(chip * rows, rows), rows)
            remote(
                summed.at[number, part],
                inbox.at[number, step - 1],
                part_send.at[0],
                part_recv.at[number],
                fellows[step - 1],
            ).start()

    def parts(number):
        return remote(
            inbox.at[number], inbox.at[number], part_send.at[0], part_recv.at[number], peer
        )

    def move(number):
        return remote(
            reduced.at[number],
            moved.at[number],
            move_send.at[0],
            move_recv.at[number],
            me.at(z=(me.z + OFFSETS[number]) % Z),
        )

    def direct():
        return remote(
            reduced.at[Z - 1],
            final.at[mine],
            last.at[0],
            last.at[1],
            me.at(z=(me.z + OFFSETS[Z - 1]) % Z, chip=me.z),
        )

    def finish(number):
        parts(number).wait_recv()
        total = summed[number, mine, :].astype(jnp.float32)
        for source in range(Z - 1):
            total = total + inbox[number, source].astype(jnp.float32)
        if number == 0:
            moved[0] = total.astype(bf16)
        else:
            reduced[number] = total.astype(bf16)
            (direct() if number == Z - 1 else move(number)).start()

    def deliver(number):
        if number:
            move(number).wait_recv()
        chip = (me.z + Z - OFFSETS[number]) % Z

        @pl.when(chip == me.chip)
        def _():
            final[mine, :] = moved[number]

        @pl.when(chip != me.chip)
        def _():
            remote(
                moved.at[number], final.at[mine], last.at[0], last.at[1], me.at(chip=chip)
            ).start()

    start_weights(0, 0)
    swap_weights(0)
    start_weights(1, 0)
    swap_weights(1)
    send_latent_kv()
    make_tables()
    send_latent_q()
    weights[0].arrive(0, 1, 0)
    start_weights(0, 1)
    weights[0].arrive(1, 1, 0)
    weights[1].arrive(0, 1, 0)
    start_weights(1, 1)
    weights[0].arrive(0, 2, 0)
    weights[0].arrive(1, 2, 0)
    send_out()
    weights[0].arrive(1, 1, 1)
    weights[0].arrive(0, 1, 1)
    send_prior()
    weights[1].arrive(1, 1, 1)
    weights[0].arrive(1, 2, 1)
    weights[1].arrive(0, 1, 1)
    weights[1].arrive(1, 1, 0)
    weights[0].arrive(0, 3, 0)
    weights[1].arrive(0, 2, 0)
    pass_prior()
    pass_latent_q()
    weights[1].arrive(1, 2, 1)
    make_keys()
    weights[0].arrive(1, 3, 1)
    weights[1].arrive(1, 2, 0)
    weights[0].arrive(0, 2, 1)
    weights[1].arrive(1, 3, 1)
    weights[1].arrive(0, 2, 1)
    weights[0].arrive(0, 4, 0)
    weights[0].arrive(1, 3, 0)
    weights[1].arrive(0, 3, 0)
    weights[0].arrive(1, 4, 1)
    weights[0].arrive(0, 3, 1)
    make_pair(0)
    attend(0, 0)
    weights[1].arrive(0, 3, 1)
    attend(0, 1)
    weights[1].arrive(1, 3, 0)
    weights[1].arrive(1, 4, 1)
    start_results(0, 0)
    weights[1].arrive(0, 4, 0)
    make_pair(1)
    attend(1, 0)
    attend(1, 1)
    start_results(1, 0)
    results[0].arrive(1, 1, 0)
    results[0].arrive(0, 1, 0)
    start_results(0, 1)
    start_results(1, 1)
    tile(0)
    results[1].arrive(1, 1, 0)
    results[0].arrive(0, 1, 1)
    results[1].arrive(0, 1, 1)
    results[0].arrive(1, 1, 1)
    results[1].arrive(0, 1, 0)
    spread(0)
    results[1].arrive(1, 1, 1)
    tile(2)
    results[1].arrive(1, 2, 0)
    tile(1)
    results[0].arrive(0, 2, 0)
    spread(2)
    results[0].arrive(1, 2, 1)
    results[0].arrive(1, 2, 0)
    finish(0)
    results[1].arrive(0, 2, 0)
    results[1].arrive(1, 2, 1)
    results[0].arrive(0, 2, 1)
    results[1].arrive(0, 2, 1)
    spread(1)
    tile(4)
    spread(4)
    results[1].arrive(1, 3, 0)
    tile(3)
    results[0].arrive(0, 3, 1)
    spread(3)
    results[0].arrive(0, 3, 0)
    results[1].arrive(0, 3, 0)
    results[0].arrive(1, 3, 1)
    finish(1)
    results[1].arrive(0, 3, 1)
    tile(5)
    results[1].arrive(1, 3, 1)
    results[0].arrive(1, 3, 0)
    spread(5)
    tile(6)
    finish(2)
    results[0].arrive(1, 4, 1)
    spread(6)
    results[0].arrive(0, 4, 0)
    finish(4)
    results[1].arrive(0, 4, 0)
    deliver(0)
    tile_ahead()
    results[1].arrive(1, 4, 1)
    tile(7)
    spread(7)
    finish(5)
    deliver(1)
    finish(6)
    finish(3)
    finish(7)
    deliver(5)
    deliver(2)
    deliver(4)
    deliver(6)
    deliver(3)
    for pair in range(2):
        group_q, group_kv = weights[pair].groups
        sends.sent(group_q, all_qw.at[pair, pl.ds(0, 15 * deep_q)], peer)
        sends.sent(group_kv, all_kvw.at[pair, pl.ds(0, 15 * deep_kv)], peer)
        sends.sent(results[pair].groups[0], every.at[pair, pl.ds(0, 7)], peer)
        sends.sent(back_groups[pair], att.at[pair, 0], peer)
    sends.sent(twin_group, given, peer)
    for group, volume in [
        (prior_group, all_kvl.at[0, :, near]),
        (lat_q_group, all_ql.at[0, near]),
        (lat_kv_group, all_kvl.at[0, :, near]),
        (twin_q_group, all_ql.at[0, near]),
        (twin_kv_group, all_kvl.at[0, :, near]),
        (twin_prior_group, all_kvl.at[0, :, near]),
        (out_group, all_ow.at[0]),
    ]:
        sends.sent(group, volume, peer)
    remote(inbox, inbox, part_send.at[0], part_recv.at[0], peer).wait_send()
    moves = moved.at[pl.ds(0, Z - 2)]
    remote(moves, moves, move_send.at[0], move_recv.at[0], peer).wait_send()
    opposite = (me.z - me.chip + Z) % Z == OFFSETS[Z - 1]
    for pick, count in ((opposite, Z), (jnp.logical_not(opposite), Z - 1)):

        @pl.when(pick)
        def _():
            volume = final.at[pl.ds(0, rows * count)]
            remote(volume, volume, last.at[0], last.at[1], peer).wait()

    out[...] = final[...]


def per_device(q_latent, kv_latent, kv_gain, q_weight, kv_weight, out_weight, documents):
    tokens = q_latent.shape[0]
    columns = out_weight.shape[1]
    ctx = lax.axis_size("ctx")
    wide_q, wide_kv = q_weight.shape[1] // 4, kv_weight.shape[1] // 4
    depth = 2 * VDIM
    part = tokens // Z
    bf16, f32 = jnp.bfloat16, jnp.float32
    spot = np.arange(128) % (ROPE // 2)
    inverse = (10000.0 ** (-2.0 * spot / ROPE)).astype(np.float32)[None, :]
    return pl.pallas_call(
        layer_kernel,
        out_shape=pltpu.VMEM((tokens, columns), bf16),
        in_specs=[HBM] * 7 + [VM],
        out_specs=VM,
        scratch_shapes=[
            pltpu.VMEM(q_weight.shape, bf16),
            pltpu.VMEM(kv_weight.shape, bf16),
            pltpu.VMEM((1, kv_gain.shape[0]), f32),
            pltpu.VMEM((1, documents.shape[0]), jnp.int32),
            pltpu.VMEM((2, tokens, q_latent.shape[1]), bf16),
            pltpu.VMEM((3, kv_latent.shape[1], tokens), bf16),
            pltpu.VMEM((2, ctx * q_weight.shape[0], wide_q), bf16),
            pltpu.VMEM((2, ctx * kv_weight.shape[0], wide_kv), bf16),
            pltpu.VMEM((2, columns, out_weight.shape[0]), bf16),
            pltpu.VMEM((1, documents.shape[0] + tokens), f32),
            pltpu.VMEM((3 * tokens, 128), f32),
            pltpu.VMEM((2, tokens, 2 * tokens), f32),
            pltpu.VMEM((3 * tokens, KL), bf16),
            pltpu.VMEM((3 * tokens, ROPE), bf16),
            pltpu.VMEM((2 * tokens, wide_q), f32),
            pltpu.VMEM((3 * tokens, wide_kv), bf16),
            pltpu.VMEM((2, 2, tokens, depth), bf16),
            pltpu.VMEM((2, Z, 2, tokens, depth), bf16),
            pltpu.VMEM((Z, tokens, columns), f32),
            pltpu.VMEM((Z, tokens, columns), bf16),
            pltpu.VMEM((Z, tokens, columns), bf16),
            pltpu.VMEM((Z, tokens, columns), bf16),
            pltpu.VMEM((Z, Z - 1, part, columns), bf16),
            pltpu.VMEM((Z, part, columns), bf16),
            pltpu.VMEM((Z, part, columns), bf16),
            pltpu.VMEM((tokens, columns), bf16),
            pltpu.VMEM((tokens, columns), f32),
            pltpu.SemaphoreType.DMA((16,)),
            pltpu.SemaphoreType.DMA((105,)),
            pltpu.SemaphoreType.DMA((7,)),
            pltpu.SemaphoreType.DMA((4,)),
            pltpu.SemaphoreType.DMA((1,)),
            pltpu.SemaphoreType.DMA((Z,)),
            pltpu.SemaphoreType.DMA((1,)),
            pltpu.SemaphoreType.DMA((Z,)),
            pltpu.SemaphoreType.DMA((2,)),
        ],
        compiler_params=pltpu.CompilerParams(
            collective_id=0, has_side_effects=True, vmem_limit_bytes=62 << 20
        ),
        name="layer",
    )(
        q_latent,
        kv_latent.T,
        q_weight,
        kv_weight,
        out_weight.T,
        kv_gain[None, :],
        documents[None, :],
        inverse,
    )


def solution(mesh):
    return jax.shard_map(
        per_device,
        mesh=mesh,
        in_specs=(
            P("ctx", None),
            P("ctx", None),
            P(),
            P("ctx", "grp"),
            P("ctx", "grp"),
            P("grp", "ctx"),
            P(),
        ),
        out_specs=P("ctx", "grp"),
        check_vma=False,
    )
```
